32 devices in a mesh: energy: 8 (over y, x, core), slab: 4 (over z).
Axes of the slice: x: 2, y: 2, z: 4, core: 2. Of those that a mesh axis runs over, the one named last changes fastest.
Arguments:
- green: bfloat16 [32, 8, 2, 128, 128], P('energy', 'slab'), may hold values from -6 to 6
- coupling: bfloat16 [8, 6, 2, 128, 128], P('slab'), may hold values from -0.1875 to 0.1875
- neighbours: int32 [8, 6], P('slab'), may hold values from 0 to 7, as said below
- shifts: int32 [2], replicated, may hold values from 1 to 4, as said below
- occupation: float32 [2], replicated, may hold values from 0.3 to 3
Outputs:
- self_energy: bfloat16 [32, 8, 2, 128, 128], P('energy', 'slab')
The draws below stay inside these ranges and needn't reach their ends.
Inputs may be any that keep to these rules, and one draw needn't show every extreme that they name: `neighbours`: each entry differs from its own atom's index by 1 to 2; column 0 differs by exactly 2. `shifts`: exactly one mode has shift 4; the others are below it.
All inputs are finite; a program needn't handle non-finite values.
Results may differ from the reference program's by a relative error of at most 0.0057.
Values may be sent and summed in bfloat16 or wider, within the bound.
A program may use at most 128 MiB of HBM per device.

```python
import math
import jax
import jax.numpy as jnp
from jax import lax

BLK = 128
NBR = 6
NMODE = 2
WID = 4
HALO = 2
NE = 32
NA = 8


def draw_neighbours(key, part):
    key_mag, key_sign = jax.random.split(jax.random.fold_in(key, 11), 2)
    magnitude = jax.random.randint(key_mag, (NA, NBR), 1, HALO + 1)
    magnitude = magnitude.at[:, 0].set(HALO)
    signs = 2 * jax.random.randint(key_sign, (NA, NBR), 0, 2) - 1
    atom_ids = jnp.arange(NA, dtype=jnp.int32)[:, None]
    forward = atom_ids + signs * magnitude
    backward = atom_ids - signs * magnitude
    inside = (forward >= 0) & (forward < NA)
    return jnp.where(inside, forward, backward).astype(jnp.int32)


def draw_shifts(key, part):
    key_vals, key_pick = jax.random.split(jax.random.fold_in(key, 23), 2)
    values = jax.random.randint(key_vals, (NMODE,), 1, WID)
    chosen = jax.random.randint(key_pick, (), 0, NMODE)
    return jnp.where(jnp.arange(NMODE) == chosen, WID, values).astype(jnp.int32)


def shard_levels(rng, dims, pieces, smallest, largest):
    factor_of, own = 1.0, jax.random.fold_in(rng, 6)
    for dim, blocks in pieces:
        heights = jnp.exp(jax.random.uniform(jax.random.fold_in(own, dim), (blocks,), jnp.float32, smallest / len(pieces), largest / len(pieces)))
        factor_of = factor_of * jnp.repeat(heights, dims[dim] // blocks).reshape([-1 if axis == dim else 1 for axis in range(len(dims))])
    return factor_of


def bell_draw(stream_key, shape, width, bound, cuts=(), kind=jnp.bfloat16):
    loudness = shard_levels(stream_key, shape, cuts, -0.22, 0.18) if cuts else 1.0
    array = jax.random.normal(stream_key, shape, jnp.float32) * width * loudness
    return jnp.minimum(jnp.maximum(array, -bound), bound).astype(kind)


def setup_inputs(seed: int = 0) -> dict:
    keys = jax.random.split(jax.random.key(seed), 6)
    green = bell_draw(keys[0], (NE, NA, 2, BLK, BLK), 1.0, 6.0, ((0, 8), (1, 4)))
    coupling = bell_draw(keys[1], (NA, NBR, NMODE, BLK, BLK), (BLK * 8) ** -0.5, 0.1875, ((0, 4),))
    neighbours = draw_neighbours(jax.random.fold_in(keys[5], 71), 0)
    shifts = draw_shifts(jax.random.fold_in(keys[5], 71), 0)
    occupation = jnp.clip(jnp.exp(jax.random.uniform(keys[4], (NMODE,), jnp.float32, math.log(0.3), math.log(3.0))), 0.3, 3.0)
    return {"green": green, "coupling": coupling, "neighbours": neighbours, "shifts": shifts, "occupation": occupation}


def atom_terms(green, coupling_row, neighbour_row, shifts, occupation):
    result = jnp.zeros((NE, 2, BLK, BLK), jnp.float32)
    for which_mode in range(NMODE):
        running = jnp.zeros((NE, 2, BLK, BLK), jnp.float32)
        for which_slot in range(NBR):
            source = lax.dynamic_index_in_dim(green, neighbour_row[which_slot].astype(jnp.int32), 1, keepdims=False).astype(jnp.float32)
            matrix = coupling_row[which_slot, which_mode].astype(jnp.float32)
            half_product = jnp.einsum("ik,erkl->eril", matrix, source).astype(jnp.bfloat16).astype(jnp.float32)
            running = running + jnp.einsum("eril,jl->erij", half_product, matrix)
        product = running.astype(jnp.bfloat16)
        padded = jnp.pad(product, ((WID, WID), (0, 0), (0, 0), (0, 0)))
        step_size = shifts[which_mode].astype(jnp.int32)
        lower = lax.dynamic_slice_in_dim(padded, (WID - step_size).astype(jnp.int32), NE, 0).astype(jnp.float32)
        upper = lax.dynamic_slice_in_dim(padded, (WID + step_size).astype(jnp.int32), NE, 0).astype(jnp.float32)
        weight = occupation[which_mode]
        result = result + (weight + 1.0) * lower + weight * upper
    return result.astype(jnp.bfloat16)


def reference(green, coupling, neighbours, shifts, occupation):
    per_atom = lax.map(lambda pair: atom_terms(green, pair[0], pair[1], shifts, occupation), (coupling, neighbours))
    return jnp.transpose(per_atom, (1, 0, 2, 3, 4))
```

```python
import functools

import jax
import jax.numpy as jnp
from jax import lax
from jax.experimental import pallas as pl
from jax.experimental.pallas import tpu as pltpu
from jax.sharding import PartitionSpec as P

WID = 4
HALO = 2
MESH = pl.DeviceIdType.MESH


def kernel(sizes, nbr_hbm, shifts_hbm, occ_hbm, green, coupling, out, *scratch):
    energies, atoms, parts, blk, slots, modes, n_energy, n_slab = sizes
    wide = [scratch[r * energies : (r + 1) * energies] for r in range(parts)]
    (coup, prod, near_send, far_send, near_recv, far_recv, own, nbr, shifts, occ,
     coup_sem, local_sem, slab_send, slab_recv, en_send, en_recv, small_sem) = scratch[parts * energies :]
    me_e = lax.axis_index("energy")
    me_s = lax.axis_index("slab")
    has_left, has_right = me_s > 0, me_s < n_slab - 1
    odd = lax.rem(me_e, 2)
    to_far = me_e - 1 + 2 * odd
    to_near = me_e + 1 - 2 * odd
    has_far = (to_far >= 0) & (to_far < n_energy)
    has_near = (to_near >= 0) & (to_near < n_energy)

    def energy_of(step):
        return step + odd * (energies - 1 - 2 * step)

    small = [
        pltpu.make_async_copy(src, dst, small_sem.at[k])
        for k, (src, dst) in enumerate(((nbr_hbm, nbr), (shifts_hbm, shifts), (occ_hbm, occ)))
    ]
    barrier = pltpu.get_barrier_semaphore()
    sides = (
        (has_left, {"slab": me_s - 1}),
        (has_right, {"slab": me_s + 1}),
        (has_far, {"energy": to_far}),
        (has_near, {"energy": to_near}),
    )
    for there, device in sides:
        @pl.when(there)
        def _(device=device):
            pl.semaphore_signal(barrier, inc=1, device_id=device, device_id_type=MESH)
    for copy in small:
        copy.start()
    coup_copy = pltpu.make_async_copy(coupling, coup, coup_sem)
    local = [
        [
            pltpu.make_async_copy(green.at[energy_of(i), :, r], wide[r][i].at[HALO : HALO + atoms], local_sem.at[r, i])
            for i in range(energies)
        ]
        for r in range(parts)
    ]
    local[0][0].start()
    coup_copy.start()
    for r in range(parts):
        for i in range(energies):
            if r or i:
                local[r][i].start()

    peers = sum(there.astype(jnp.int32) for there, _ in sides)
    pl.semaphore_wait(barrier, peers)

    def slab_copy(r, i, direction):
        halo, e = wide[r][i], energy_of(i)
        if direction == 0:
            src, dst, to = green.at[e, atoms - HALO : atoms, r], halo.at[0:HALO], me_s + 1
        else:
            src, dst, to = green.at[e, 0:HALO, r], halo.at[HALO + atoms : 2 * HALO + atoms], me_s - 1
        return pltpu.make_async_remote_copy(
            src_ref=src,
            dst_ref=dst,
            send_sem=slab_send.at[direction, r, i],
            recv_sem=slab_recv.at[direction, r, i],
            device_id={"slab": to},
            device_id_type=MESH,
        )

    for r in range(parts):
        for i in range(energies):
            @pl.when(has_right)
            def _(i=i, r=r):
                slab_copy(r, i, 0).start()
            @pl.when(has_left)
            def _(i=i, r=r):
                slab_copy(r, i, 1).start()

    def energy_copy(r, u, direction):
        if direction == 0:
            src, dst, to = far_send.at[r, u], far_recv.at[r, u], to_far
        else:
            src, dst, to = near_send.at[r, u], near_recv.at[r, u], to_near
        return pltpu.make_async_remote_copy(
            src_ref=src,
            dst_ref=dst,
            send_sem=en_send.at[direction, r, u],
            recv_sem=en_recv.at[direction, r, u],
            device_id={"energy": to},
            device_id_type=MESH,
        )

    @pl.when(jnp.logical_not(has_far))
    def _():
        far_recv[...] = jnp.zeros_like(far_recv)
    @pl.when(jnp.logical_not(has_near))
    def _():
        near_recv[...] = jnp.zeros_like(near_recv)

    first_atom = me_s * atoms

    def products(r, i):
        def body(a, carry):
            halves, mats = [], []
            for j in range(slots):
                g = wide[r][i][jnp.clip(nbr[a, j] - first_atom + HALO, 0, atoms + 2 * HALO - 1)]
                c = coup[a, j]
                mats.append(c)
                h = jnp.dot(c.reshape(modes * blk, blk), g, preferred_element_type=jnp.float32)
                halves.append(h.astype(jnp.bfloat16))
            for m in range(modes):
                lhs = jnp.concatenate([h[m * blk : (m + 1) * blk] for h in halves], axis=1)
                rhs = jnp.concatenate([c[m] for c in mats], axis=1)
                p = lax.dot_general(lhs, rhs, (((1,), (1,)), ((), ())), preferred_element_type=jnp.float32)
                prod[m, r, i, a] = p.astype(jnp.bfloat16)
            return carry

        lax.fori_loop(0, atoms, body, 0)

    def store_sum(target, r, u, terms):
        def body(a, carry):
            total = None
            for m, index, weight in terms:
                inside = (index >= 0) & (index < energies)
                safe = jnp.clip(index, 0, energies - 1)
                term = jnp.where(inside, weight, 0.0) * prod[m, r, safe, a].astype(jnp.float32)
                total = term if total is None else total + term
            target[r, u, a] = total.astype(target.dtype)
            return carry

        lax.fori_loop(0, atoms, body, 0)

    odd_f = odd.astype(jnp.float32)

    def toward_far(m):
        return occ[m] + odd_f

    def toward_near(m):
        return occ[m] + (1.0 - odd_f)

    def own_sums(r):
        for t in range(energies):
            terms = []
            for m in range(modes):
                terms.append((m, t - shifts[m], toward_near(m)))
                terms.append((m, t + shifts[m], toward_far(m)))
            store_sum(own, r, t, terms)

    def finish(r, t):
        far_u = WID - 1 - t if t < WID else None
        near_u = energies - 1 - t if t >= energies - WID else None
        if near_u is not None:
            @pl.when(has_near)
            def _():
                energy_copy(r, near_u, 1).wait_recv()
        if far_u is not None:
            @pl.when(has_far)
            def _():
                energy_copy(r, far_u, 0).wait_recv()
        e = energy_of(t)

        def body(a, carry):
            total = own[r, t, a]
            if far_u is not None:
                total = total + far_recv[r, far_u, a].astype(jnp.float32)
            if near_u is not None:
                total = total + near_recv[r, near_u, a].astype(jnp.float32)
            out[e, a, r] = total.astype(jnp.bfloat16)
            return carry

        lax.fori_loop(0, atoms, body, 0)

    for r in range(parts):
        for i in range(energies):
            local[r][i].wait()
            if r == 0 and i == 0:
                coup_copy.wait()
                for copy in small:
                    copy.wait()
            @pl.when(has_left)
            def _(i=i, r=r):
                slab_copy(r, i, 0).wait_recv()
            @pl.when(has_right)
            def _(i=i, r=r):
                slab_copy(r, i, 1).wait_recv()
            products(r, i)
            if i < WID:
                @pl.when(has_far)
                def _(u=i, r=r):
                    store_sum(far_send, r, u, [(m, u - WID + shifts[m], toward_far(m)) for m in range(modes)])
                    energy_copy(r, u, 0).start()
        for u in range(WID):
            @pl.when(has_near)
            def _(u=u, r=r):
                store_sum(near_send, r, u, [(m, energies + u - shifts[m], toward_near(m)) for m in range(modes)])
                energy_copy(r, u, 1).start()
        own_sums(r)

    for r in range(parts):
        for t in reversed(range(energies)):
            finish(r, t)

    for r in range(parts):
        for i in range(energies):
            @pl.when(has_right)
            def _(i=i, r=r):
                slab_copy(r, i, 0).wait_send()
            @pl.when(has_left)
            def _(i=i, r=r):
                slab_copy(r, i, 1).wait_send()
        for u in range(WID):
            @pl.when(has_far)
            def _(u=u, r=r):
                energy_copy(r, u, 0).wait_send()
            @pl.when(has_near)
            def _(u=u, r=r):
                energy_copy(r, u, 1).wait_send()


def solution(mesh):
    def shards(green, coupling, neighbours, shifts, occupation):
        energies, atoms, parts, blk, _ = green.shape
        slots, modes = coupling.shape[1:3]
        sizes = (energies, atoms, parts, blk, slots, modes, mesh.shape["energy"], mesh.shape["slab"])
        bf16, f32 = jnp.bfloat16, jnp.float32
        hbm = pl.BlockSpec(memory_space=pltpu.HBM)
        edge = (parts, WID, atoms, blk, blk)
        dma = pltpu.SemaphoreType.DMA
        return pl.pallas_call(
            functools.partial(kernel, sizes),
            out_shape=pltpu.VMEM(green.shape, bf16),
            in_specs=[hbm] * 5,
            out_specs=pl.BlockSpec(memory_space=pltpu.VMEM),
            scratch_shapes=[pltpu.VMEM((atoms + 2 * HALO, blk, blk), bf16) for _ in range(parts * energies)]
            + [
                pltpu.VMEM(coupling.shape, bf16),
                pltpu.VMEM((modes, parts, energies, atoms, blk, blk), bf16),
                pltpu.VMEM(edge, bf16),
                pltpu.VMEM(edge, bf16),
                pltpu.VMEM(edge, bf16),
                pltpu.VMEM(edge, bf16),
                pltpu.VMEM((parts, energies, atoms, blk, blk), f32),
                pltpu.SMEM((atoms, slots), jnp.int32),
                pltpu.SMEM((modes,), jnp.int32),
                pltpu.SMEM((modes,), f32),
                dma,
                dma((parts, energies)),
                dma((2, parts, energies)),
                dma((2, parts, energies)),
                dma((2, parts, WID)),
                dma((2, parts, WID)),
                dma((3,)),
            ],
            compiler_params=pltpu.CompilerParams(collective_id=0, has_side_effects=True),
        )(neighbours, shifts, occupation, green, coupling)

    return jax.shard_map(
        shards,
        mesh=mesh,
        in_specs=(
            P("energy", "slab", None, None, None),
            P("slab", None, None, None, None),
            P("slab", None),
            P(),
            P(),
        ),
        out_specs=P("energy", "slab", None, None, None),
        check_vma=False,
    )
```

```python
import functools

import jax
import jax.numpy as jnp
from jax import lax
from jax.experimental import pallas as pl
from jax.experimental.pallas import tpu as pltpu
from jax.sharding import PartitionSpec as P

WID = 4
HALO = 2
MESH = pl.DeviceIdType.MESH


def kernel(sizes, nbr_hbm, shifts_hbm, occ_hbm, green, coupling, out, *scratch):
    energies, atoms, parts, blk, slots, modes, n_energy, n_slab = sizes
    wide = [scratch[r * energies : (r + 1) * energies] for r in range(parts)]
    foreign = scratch[parts * energies]
    (coup, prod, near_send, far_send, near_recv, far_recv, own, nbr, shifts, occ,
     coup_sem, local_sem, slab_send, slab_recv, en_send, en_recv, small_sem, prod_f, raw_send, raw_recv,
     pass_send, pass_recv) = scratch[parts * energies + 1 :]
    me_e = lax.axis_index("energy")
    me_s = lax.axis_index("slab")
    has_left, has_right = me_s > 0, me_s < n_slab - 1
    odd = lax.rem(me_e, 2)
    to_far = me_e - 1 + 2 * odd
    to_near = me_e + 1 - 2 * odd
    has_far = (to_far >= 0) & (to_far < n_energy)
    has_near = (to_near >= 0) & (to_near < n_energy)

    def energy_of(step):
        return step + odd * (energies - 1 - 2 * step)

    last, late = parts - 1, 0
    orders = [list(range(energies)) for _ in range(parts)]
    orders[last] = [i for i in range(energies) if i != late] + [late]

    def far_units(r):
        return [u for u in range(WID) if r != last or u != late]

    small = [
        pltpu.make_async_copy(src, dst, small_sem.at[k])
        for k, (src, dst) in enumerate(((nbr_hbm, nbr), (shifts_hbm, shifts), (occ_hbm, occ)))
    ]
    barrier = pltpu.get_barrier_semaphore()
    sides = (
        (has_left, {"slab": me_s - 1}),
        (has_right, {"slab": me_s + 1}),
        (has_far, {"energy": to_far}),
        (has_near, {"energy": to_near}),
    )
    for there, device in sides:
        @pl.when(there)
        def _(device=device):
            pl.semaphore_signal(barrier, inc=1, device_id=device, device_id_type=MESH)
    for copy in small:
        copy.start()
    coup_copy = pltpu.make_async_copy(coupling, coup, coup_sem)
    local = [
        [
            pltpu.make_async_copy(green.at[energy_of(i), :, r], wide[r][i].at[HALO : HALO + atoms], local_sem.at[r, i])
            for i in range(energies)
        ]
        for r in range(parts)
    ]
    local[0][0].start()
    coup_copy.start()
    for r in range(parts):
        for i in range(energies):
            if r or i:
                local[r][i].start()

    peers = sum(there.astype(jnp.int32) for there, _ in sides)
    pl.semaphore_wait(barrier, peers)

    def slab_copy(r, i, direction):
        halo, e = wide[r][i], energy_of(i)
        if direction == 0:
            src, dst, to = green.at[e, atoms - HALO : atoms, r], halo.at[0:HALO], me_s + 1
        else:
            src, dst, to = green.at[e, 0:HALO, r], halo.at[HALO + atoms : 2 * HALO + atoms], me_s - 1
        return pltpu.make_async_remote_copy(
            src_ref=src,
            dst_ref=dst,
            send_sem=slab_send.at[direction, r, i],
            recv_sem=slab_recv.at[direction, r, i],
            device_id={"slab": to},
            device_id_type=MESH,
        )

    raw_copy = pltpu.make_async_remote_copy(
        src_ref=green.at[energy_of(late), :, last],
        dst_ref=foreign.at[HALO : HALO + atoms],
        send_sem=raw_send,
        recv_sem=raw_recv,
        device_id={"energy": to_far},
        device_id_type=MESH,
    )

    def pass_copy(direction):
        if direction == 0:
            src, dst, to = foreign.at[atoms : HALO + atoms], foreign.at[0:HALO], me_s + 1
        else:
            src, dst, to = foreign.at[HALO : 2 * HALO], foreign.at[HALO + atoms : 2 * HALO + atoms], me_s - 1
        return pltpu.make_async_remote_copy(
            src_ref=src,
            dst_ref=dst,
            send_sem=pass_send.at[direction],
            recv_sem=pass_recv.at[direction],
            device_id={"slab": to},
            device_id_type=MESH,
        )

    @pl.when(has_far)
    def _():
        raw_copy.start()

    for r in range(parts):
        for i in orders[r]:
            @pl.when(has_right)
            def _(i=i, r=r):
                slab_copy(r, i, 0).start()
            @pl.when(has_left)
            def _(i=i, r=r):
                slab_copy(r, i, 1).start()

    def energy_copy(r, u, direction):
        if direction == 0:
            src, dst, to = far_send.at[r, u], far_recv.at[r, u], to_far
        else:
            src, dst, to = near_send.at[r, u], near_recv.at[r, u], to_near
        return pltpu.make_async_remote_copy(
            src_ref=src,
            dst_ref=dst,
            send_sem=en_send.at[direction, r, u],
            recv_sem=en_recv.at[direction, r, u],
            device_id={"energy": to},
            device_id_type=MESH,
        )

    @pl.when(jnp.logical_not(has_far))
    def _():
        far_recv[...] = jnp.zeros_like(far_recv)
    @pl.when(jnp.logical_not(has_near))
    def _():
        near_recv[...] = jnp.zeros_like(near_recv)

    first_atom = me_s * atoms

    def products(source, store):
        halves, mats = [], []
        for a in range(atoms):
            mats.append([coup[a, j] for j in range(slots)])
            halves.append([])
            for j in range(slots):
                g = source[jnp.clip(nbr[a, j] - first_atom + HALO, 0, atoms + 2 * HALO - 1)]
                h = jnp.dot(mats[a][j].reshape(modes * blk, blk), g, preferred_element_type=jnp.float32)
                halves[a].append(h.astype(jnp.bfloat16))
        for a in range(atoms):
            for m in range(modes):
                lhs = jnp.concatenate([h[m * blk : (m + 1) * blk] for h in halves[a]], axis=1)
                rhs = jnp.concatenate([c[m] for c in mats[a]], axis=1)
                p = lax.dot_general(lhs, rhs, (((1,), (1,)), ((), ())), preferred_element_type=jnp.float32)
                store(m, a, p.astype(jnp.bfloat16))

    def store_sum(target, r, u, terms, spare=0, but=None):
        def body(a, carry):
            total = None
            for m, index, weight in terms:
                inside = (index >= 0) & (index < energies)
                if but is not None:
                    inside = inside & (index != but)
                safe = jnp.where(inside, index, spare)
                term = jnp.where(inside, weight, 0.0) * prod[m, r, safe, a].astype(jnp.float32)
                total = term if total is None else total + term
            target[r, u, a] = total.astype(target.dtype)
            return carry

        lax.fori_loop(0, atoms, body, 0)

    odd_f = odd.astype(jnp.float32)

    def toward_far(m):
        return occ[m] + odd_f

    def toward_near(m):
        return occ[m] + (1.0 - odd_f)

    def own_sums(r, but=None):
        for t in range(energies):
            terms = []
            for m in range(modes):
                terms.append((m, t - shifts[m], toward_near(m)))
                terms.append((m, t + shifts[m], toward_far(m)))
            store_sum(own, r, t, terms, orders[r][0], but)

    def finish(r, t):
        far_u = WID - 1 - t if WID - 1 - t in far_units(r) else None
        near_u = energies - 1 - t if t >= energies - WID else None
        if near_u is not None:
            @pl.when(has_near)
            def _():
                energy_copy(r, near_u, 1).wait_recv()
        if far_u is not None:
            @pl.when(has_far)
            def _():
                energy_copy(r, far_u, 0).wait_recv()
        e = energy_of(t)

        def body(a, carry):
            total = own[r, t, a]
            if far_u is not None:
                total = total + far_recv[r, far_u, a].astype(jnp.float32)
            if near_u is not None:
                total = total + near_recv[r, near_u, a].astype(jnp.float32)
            if r == last:
                for m in range(modes):
                    if t != late and abs(t - late) <= WID:
                        weight = jnp.where(shifts[m] == abs(t - late), toward_near(m) if t > late else toward_far(m), 0.0)
                        total = total + weight * prod[m, r, late, a].astype(jnp.float32)
                    if t + 1 + late <= WID:
                        weight = jnp.where(shifts[m] == t + 1 + late, toward_near(m), 0.0)
                        total = total + weight * prod_f[m, a].astype(jnp.float32)
            out[e, a, r] = total.astype(jnp.bfloat16)
            return carry

        lax.fori_loop(0, atoms, body, 0)

    for r in range(parts):
        done, sent = set(), set()
        for i in orders[r]:
            if r == last and i == late:
                own_sums(r, late)
            local[r][i].wait()
            if r == 0 and not done:
                coup_copy.wait()
                for copy in small:
                    copy.wait()
            @pl.when(has_left)
            def _(i=i, r=r):
                slab_copy(r, i, 0).wait_recv()
            @pl.when(has_right)
            def _(i=i, r=r):
                slab_copy(r, i, 1).wait_recv()

            def store(m, a, value, r=r, i=i):
                prod[m, r, i, a] = value

            products(wide[r][i], store)
            done.add(i)
            for u in far_units(r):
                needed = {k for k in range(u - WID + 1, u + 1) if k >= 0 and not (r == last and k == late)}
                if u not in sent and needed <= done:
                    sent.add(u)
                    @pl.when(has_far)
                    def _(u=u, r=r):
                        store_sum(
                            far_send, r, u, [(m, u - WID + shifts[m], toward_far(m)) for m in range(modes)],
                            u, late if r == last else None,
                        )
                        energy_copy(r, u, 0).start()
            if r == 0 and len(done) == 1:
                @pl.when(has_far)
                def _():
                    raw_copy.wait_recv()
                    @pl.when(has_right)
                    def _():
                        pass_copy(0).start()
                    @pl.when(has_left)
                    def _():
                        pass_copy(1).start()
        for u in range(WID):
            @pl.when(has_near)
            def _(u=u, r=r):
                store_sum(near_send, r, u, [(m, energies + u - shifts[m], toward_near(m)) for m in range(modes)])
                energy_copy(r, u, 1).start()
        if r < last:
            own_sums(r)

    for r in range(last):
        for t in reversed(range(energies)):
            finish(r, t)

    @pl.when(has_far)
    def _():
        @pl.when(has_left)
        def _():
            pass_copy(0).wait_recv()
        @pl.when(has_right)
        def _():
            pass_copy(1).wait_recv()

        def store(m, a, value):
            prod_f[m, a] = value

        products(foreign, store)

    @pl.when(jnp.logical_not(has_far))
    def _():
        prod_f[...] = jnp.zeros_like(prod_f)

    for t in reversed(range(energies)):
        finish(last, t)

    @pl.when(has_far)
    def _():
        raw_copy.wait_send()
        @pl.when(has_right)
        def _():
            pass_copy(0).wait_send()
        @pl.when(has_left)
        def _():
            pass_copy(1).wait_send()

    for r in range(parts):
        for i in range(energies):
            @pl.when(has_right)
            def _(i=i, r=r):
                slab_copy(r, i, 0).wait_send()
            @pl.when(has_left)
            def _(i=i, r=r):
                slab_copy(r, i, 1).wait_send()
        for u in far_units(r):
            @pl.when(has_far)
            def _(u=u, r=r):
                energy_copy(r, u, 0).wait_send()
        for u in range(WID):
            @pl.when(has_near)
            def _(u=u, r=r):
                energy_copy(r, u, 1).wait_send()


def solution(mesh):
    def shards(green, coupling, neighbours, shifts, occupation):
        energies, atoms, parts, blk, _ = green.shape
        slots, modes = coupling.shape[1:3]
        sizes = (energies, atoms, parts, blk, slots, modes, mesh.shape["energy"], mesh.shape["slab"])
        bf16, f32 = jnp.bfloat16, jnp.float32
        hbm = pl.BlockSpec(memory_space=pltpu.HBM)
        edge = (parts, WID, atoms, blk, blk)
        dma = pltpu.SemaphoreType.DMA
        return pl.pallas_call(
            functools.partial(kernel, sizes),
            out_shape=pltpu.VMEM(green.shape, bf16),
            in_specs=[hbm] * 5,
            out_specs=pl.BlockSpec(memory_space=pltpu.VMEM),
            scratch_shapes=[pltpu.VMEM((atoms + 2 * HALO, blk, blk), bf16) for _ in range(parts * energies + 1)]
            + [
                pltpu.VMEM(coupling.shape, bf16),
                pltpu.VMEM((modes, parts, energies, atoms, blk, blk), bf16),
                pltpu.VMEM(edge, bf16),
                pltpu.VMEM(edge, bf16),
                pltpu.VMEM(edge, bf16),
                pltpu.VMEM(edge, bf16),
                pltpu.VMEM((parts, energies, atoms, blk, blk), f32),
                pltpu.SMEM((atoms, slots), jnp.int32),
                pltpu.SMEM((modes,), jnp.int32),
                pltpu.SMEM((modes,), f32),
                dma,
                dma((parts, energies)),
                dma((2, parts, energies)),
                dma((2, parts, energies)),
                dma((2, parts, WID)),
                dma((2, parts, WID)),
                dma((3,)),
                pltpu.VMEM((modes, atoms, blk, blk), bf16),
                dma,
                dma,
                dma((2,)),
                dma((2,)),
            ],
            compiler_params=pltpu.CompilerParams(collective_id=0, has_side_effects=True),
        )(neighbours, shifts, occupation, green, coupling)

    return jax.shard_map(
        shards,
        mesh=mesh,
        in_specs=(
            P("energy", "slab", None, None, None),
            P("slab", None, None, None, None),
            P("slab", None),
            P(),
            P(),
        ),
        out_specs=P("energy", "slab", None, None, None),
        check_vma=False,
    )
```

```python
import functools

import jax
import jax.numpy as jnp
from jax import lax
from jax.experimental import pallas as pl
from jax.experimental.pallas import tpu as pltpu
from jax.sharding import PartitionSpec as P

WID = 4
HALO = 2
MESH = pl.DeviceIdType.MESH


def kernel(sizes, nbr_hbm, shifts_hbm, occ_hbm, green, coupling, out, *scratch):
    energies, atoms, parts, blk, slots, modes, n_energy, n_slab = sizes
    wide = [scratch[r * energies : (r + 1) * energies] for r in range(parts)]
    foreign = scratch[parts * energies]
    (coup, prod, near_send, far_send, near_recv, far_recv, own, nbr, shifts, occ,
     coup_sem, local_sem, slab_send, slab_recv, en_send, en_recv, small_sem, prod_f, raw_send, raw_recv,
     pass_send, pass_recv, right_in, energy_in) = scratch[parts * energies + 1 :]
    me_e = lax.axis_index("energy")
    me_s = lax.axis_index("slab")
    has_left, has_right = me_s > 0, me_s < n_slab - 1
    odd = lax.rem(me_e, 2)
    to_far = me_e - 1 + 2 * odd
    to_near = me_e + 1 - 2 * odd
    has_far = (to_far >= 0) & (to_far < n_energy)
    has_near = (to_near >= 0) & (to_near < n_energy)

    def energy_of(step):
        return step + odd * (energies - 1 - 2 * step)

    last, late = parts - 1, 0
    orders = [list(range(energies)) for _ in range(parts)]
    orders[last] = [i for i in range(energies) if i != late] + [late]

    def far_units(r):
        return [u for u in range(WID) if r != last or u != late]

    small = [
        pltpu.make_async_copy(src, dst, small_sem.at[k])
        for k, (src, dst) in enumerate(((nbr_hbm, nbr), (shifts_hbm, shifts), (occ_hbm, occ)))
    ]
    has_prev, has_next = me_e > 0, me_e < n_energy - 1
    barrier = pltpu.get_barrier_semaphore()

    def tell(there, sem, device):
        @pl.when(there)
        def _():
            pl.semaphore_signal(sem, inc=1, device_id=device, device_id_type=MESH)

    tell(has_right, barrier, {"slab": me_s + 1})
    uneven = lax.rem(me_e, 2)
    energy_peers = has_prev.astype(jnp.int32) + has_next.astype(jnp.int32)
    for there, device in ((has_prev, {"energy": me_e - 1}), (has_next, {"energy": me_e + 1})):
        tell(there & (uneven == 1), barrier, device)
    for copy in small:
        copy.start()
    coup_copy = pltpu.make_async_copy(coupling, coup, coup_sem)
    local = [
        [
            pltpu.make_async_copy(green.at[energy_of(i), :, r], wide[r][i].at[HALO : HALO + atoms], local_sem.at[r, i])
            for i in range(energies)
        ]
        for r in range(parts)
    ]
    local[0][0].start()
    coup_copy.start()
    for r in range(parts):
        for i in range(energies):
            if r or i:
                local[r][i].start()

    entered = has_left.astype(jnp.int32) + (1 - uneven) * energy_peers

    @pl.when(entered > 0)
    def _():
        pl.semaphore_wait(barrier, entered)

    tell(has_left, right_in, {"slab": me_s - 1})
    for there, device in ((has_prev, {"energy": me_e - 1}), (has_next, {"energy": me_e + 1})):
        tell(there & (uneven == 0), energy_in, device)

    def slab_copy(r, i, direction):
        halo, e = wide[r][i], energy_of(i)
        if direction == 0:
            src, dst, to = green.at[e, atoms - HALO : atoms, r], halo.at[0:HALO], me_s + 1
        else:
            src, dst, to = green.at[e, 0:HALO, r], halo.at[HALO + atoms : 2 * HALO + atoms], me_s - 1
        return pltpu.make_async_remote_copy(
            src_ref=src,
            dst_ref=dst,
            send_sem=slab_send.at[direction, r, i],
            recv_sem=slab_recv.at[direction, r, i],
            device_id={"slab": to},
            device_id_type=MESH,
        )

    raw_copy = pltpu.make_async_remote_copy(
        src_ref=green.at[energy_of(late), :, last],
        dst_ref=foreign.at[HALO : HALO + atoms],
        send_sem=raw_send,
        recv_sem=raw_recv,
        device_id={"energy": to_far},
        device_id_type=MESH,
    )

    def pass_copy(direction):
        if direction == 0:
            src, dst, to = foreign.at[atoms : HALO + atoms], foreign.at[0:HALO], me_s + 1
        else:
            src, dst, to = foreign.at[HALO : 2 * HALO], foreign.at[HALO + atoms : 2 * HALO + atoms], me_s - 1
        return pltpu.make_async_remote_copy(
            src_ref=src,
            dst_ref=dst,
            send_sem=pass_send.at[direction],
            recv_sem=pass_recv.at[direction],
            device_id={"slab": to},
            device_id_type=MESH,
        )

    @pl.when(has_left)
    def _():
        for r in range(parts):
            for i in orders[r]:
                slab_copy(r, i, 1).start()
    @pl.when(has_right)
    def _():
        pl.semaphore_wait(right_in, 1)
        for r in range(parts):
            for i in orders[r]:
                slab_copy(r, i, 0).start()

    @pl.when(uneven * energy_peers > 0)
    def _():
        pl.semaphore_wait(energy_in, energy_peers)

    @pl.when(has_far)
    def _():
        raw_copy.start()

    def energy_copy(r, u, direction):
        if direction == 0:
            src, dst, to = far_send.at[r, u], far_recv.at[r, u], to_far
        else:
            src, dst, to = near_send.at[r, u], near_recv.at[r, u], to_near
        return pltpu.make_async_remote_copy(
            src_ref=src,
            dst_ref=dst,
            send_sem=en_send.at[direction, r, u],
            recv_sem=en_recv.at[direction, r, u],
            device_id={"energy": to},
            device_id_type=MESH,
        )

    @pl.when(jnp.logical_not(has_far))
    def _():
        far_recv[...] = jnp.zeros_like(far_recv)
    @pl.when(jnp.logical_not(has_near))
    def _():
        near_recv[...] = jnp.zeros_like(near_recv)

    first_atom = me_s * atoms

    def products(source, store):
        halves, mats = [], []
        for a in range(atoms):
            mats.append([coup[a, j] for j in range(slots)])
            halves.append([])
            for j in range(slots):
                g = source[jnp.clip(nbr[a, j] - first_atom + HALO, 0, atoms + 2 * HALO - 1)]
                h = jnp.dot(mats[a][j].reshape(modes * blk, blk), g, preferred_element_type=jnp.float32)
                halves[a].append(h.astype(jnp.bfloat16))
        for a in range(atoms):
            for m in range(modes):
                lhs = jnp.concatenate([h[m * blk : (m + 1) * blk] for h in halves[a]], axis=1)
                rhs = jnp.concatenate([c[m] for c in mats[a]], axis=1)
                p = lax.dot_general(lhs, rhs, (((1,), (1,)), ((), ())), preferred_element_type=jnp.float32)
                store(m, a, p.astype(jnp.bfloat16))

    def store_sum(target, r, u, terms, spare=0, but=None):
        def body(a, carry):
            total = None
            for m, index, weight in terms:
                inside = (index >= 0) & (index < energies)
                if but is not None:
                    inside = inside & (index != but)
                safe = jnp.where(inside, index, spare)
                term = jnp.where(inside, weight, 0.0) * prod[m, r, safe, a].astype(jnp.float32)
                total = term if total is None else total + term
            target[r, u, a] = total.astype(target.dtype)
            return carry

        lax.fori_loop(0, atoms, body, 0)

    odd_f = odd.astype(jnp.float32)

    def toward_far(m):
        return occ[m] + odd_f

    def toward_near(m):
        return occ[m] + (1.0 - odd_f)

    def own_sums(r, but=None):
        for t in range(energies):
            terms = []
            for m in range(modes):
                terms.append((m, t - shifts[m], toward_near(m)))
                terms.append((m, t + shifts[m], toward_far(m)))
            store_sum(own, r, t, terms, orders[r][0], but)

    def finish(r, t):
        far_u = WID - 1 - t if WID - 1 - t in far_units(r) else None
        near_u = energies - 1 - t if t >= energies - WID else None
        if near_u is not None:
            @pl.when(has_near)
            def _():
                energy_copy(r, near_u, 1).wait_recv()
        if far_u is not None:
            @pl.when(has_far)
            def _():
                energy_copy(r, far_u, 0).wait_recv()
        e = energy_of(t)

        def body(a, carry):
            total = own[r, t, a]
            if far_u is not None:
                total = total + far_recv[r, far_u, a].astype(jnp.float32)
            if near_u is not None:
                total = total + near_recv[r, near_u, a].astype(jnp.float32)
            if r == last:
                for m in range(modes):
                    if t != late and abs(t - late) <= WID:
                        weight = jnp.where(shifts[m] == abs(t - late), toward_near(m) if t > late else toward_far(m), 0.0)
                        total = total + weight * prod[m, r, late, a].astype(jnp.float32)
                    if t + 1 + late <= WID:
                        weight = jnp.where(shifts[m] == t + 1 + late, toward_near(m), 0.0)
                        total = total + weight * prod_f[m, a].astype(jnp.float32)
            out[e, a, r] = total.astype(jnp.bfloat16)
            return carry

        lax.fori_loop(0, atoms, body, 0)

    for r in range(parts):
        done, sent = set(), set()
        for i in orders[r]:
            if r == last and i == late:
                own_sums(r, late)
            local[r][i].wait()
            if r == 0 and not done:
                coup_copy.wait()
                for copy in small:
                    copy.wait()
            @pl.when(has_left)
            def _(i=i, r=r):
                slab_copy(r, i, 0).wait_recv()
            @pl.when(has_right)
            def _(i=i, r=r):
                slab_copy(r, i, 1).wait_recv()

            def store(m, a, value, r=r, i=i):
                prod[m, r, i, a] = value

            products(wide[r][i], store)
            done.add(i)
            for u in far_units(r):
                needed = {k for k in range(u - WID + 1, u + 1) if k >= 0 and not (r == last and k == late)}
                if u not in sent and needed <= done:
                    sent.add(u)
                    @pl.when(has_far)
                    def _(u=u, r=r):
                        store_sum(
                            far_send, r, u, [(m, u - WID + shifts[m], toward_far(m)) for m in range(modes)],
                            u, late if r == last else None,
                        )
                        energy_copy(r, u, 0).start()
            if r == 0 and len(done) == 1:
                @pl.when(has_far)
                def _():
                    raw_copy.wait_recv()
                    @pl.when(has_right)
                    def _():
                        pass_copy(0).start()
                    @pl.when(has_left)
                    def _():
                        pass_copy(1).start()
        for u in range(WID):
            @pl.when(has_near)
            def _(u=u, r=r):
                store_sum(near_send, r, u, [(m, energies + u - shifts[m], toward_near(m)) for m in range(modes)])
                energy_copy(r, u, 1).start()
        if r < last:
            own_sums(r)

    for r in range(last):
        for t in reversed(range(energies)):
            finish(r, t)

    @pl.when(has_far)
    def _():
        @pl.when(has_left)
        def _():
            pass_copy(0).wait_recv()
        @pl.when(has_right)
        def _():
            pass_copy(1).wait_recv()

        def store(m, a, value):
            prod_f[m, a] = value

        products(foreign, store)

    @pl.when(jnp.logical_not(has_far))
    def _():
        prod_f[...] = jnp.zeros_like(prod_f)

    for t in reversed(range(energies)):
        finish(last, t)

    @pl.when(has_far)
    def _():
        raw_copy.wait_send()
        @pl.when(has_right)
        def _():
            pass_copy(0).wait_send()
        @pl.when(has_left)
        def _():
            pass_copy(1).wait_send()

    for r in range(parts):
        for i in range(energies):
            @pl.when(has_right)
            def _(i=i, r=r):
                slab_copy(r, i, 0).wait_send()
            @pl.when(has_left)
            def _(i=i, r=r):
                slab_copy(r, i, 1).wait_send()
        for u in far_units(r):
            @pl.when(has_far)
            def _(u=u, r=r):
                energy_copy(r, u, 0).wait_send()
        for u in range(WID):
            @pl.when(has_near)
            def _(u=u, r=r):
                energy_copy(r, u, 1).wait_send()


def solution(mesh):
    def shards(green, coupling, neighbours, shifts, occupation):
        energies, atoms, parts, blk, _ = green.shape
        slots, modes = coupling.shape[1:3]
        sizes = (energies, atoms, parts, blk, slots, modes, mesh.shape["energy"], mesh.shape["slab"])
        bf16, f32 = jnp.bfloat16, jnp.float32
        hbm = pl.BlockSpec(memory_space=pltpu.HBM)
        edge = (parts, WID, atoms, blk, blk)
        dma = pltpu.SemaphoreType.DMA
        return pl.pallas_call(
            functools.partial(kernel, sizes),
            out_shape=pltpu.VMEM(green.shape, bf16),
            in_specs=[hbm] * 5,
            out_specs=pl.BlockSpec(memory_space=pltpu.VMEM),
            scratch_shapes=[pltpu.VMEM((atoms + 2 * HALO, blk, blk), bf16) for _ in range(parts * energies + 1)]
            + [
                pltpu.VMEM(coupling.shape, bf16),
                pltpu.VMEM((modes, parts, energies, atoms, blk, blk), bf16),
                pltpu.VMEM(edge, bf16),
                pltpu.VMEM(edge, bf16),
                pltpu.VMEM(edge, bf16),
                pltpu.VMEM(edge, bf16),
                pltpu.VMEM((parts, energies, atoms, blk, blk), f32),
                pltpu.SMEM((atoms, slots), jnp.int32),
                pltpu.SMEM((modes,), jnp.int32),
                pltpu.SMEM((modes,), f32),
                dma,
                dma((parts, energies)),
                dma((2, parts, energies)),
                dma((2, parts, energies)),
                dma((2, parts, WID)),
                dma((2, parts, WID)),
                dma((3,)),
                pltpu.VMEM((modes, atoms, blk, blk), bf16),
                dma,
                dma,
                dma((2,)),
                dma((2,)),
                pltpu.SemaphoreType.REGULAR,
                pltpu.SemaphoreType.REGULAR,
            ],
            compiler_params=pltpu.CompilerParams(collective_id=0, has_side_effects=True),
        )(neighbours, shifts, occupation, green, coupling)

    return jax.shard_map(
        shards,
        mesh=mesh,
        in_specs=(
            P("energy", "slab", None, None, None),
            P("slab", None, None, None, None),
            P("slab", None),
            P(),
            P(),
        ),
        out_specs=P("energy", "slab", None, None, None),
        check_vma=False,
    )
```

```python
import functools

import jax
import jax.numpy as jnp
from jax import lax
from jax.experimental import pallas as pl
from jax.experimental.pallas import tpu as pltpu
from jax.sharding import PartitionSpec as P

WID = 4
HALO = 2
MESH = pl.DeviceIdType.MESH


def kernel(sizes, nbr_hbm, shifts_hbm, occ_hbm, green, coupling, out, *scratch):
    energies, atoms, parts, blk, slots, modes, n_energy, n_slab = sizes
    wide = [scratch[r * energies : (r + 1) * energies] for r in range(parts)]
    foreign = scratch[parts * energies : parts * energies + 2]
    (coup, prod, near_send, far_send, near_recv, far_recv, own, nbr, shifts, occ,
     coup_sem, local_sem, slab_send, slab_recv, en_send, en_recv, small_sem, prod_f, raw_send, raw_recv,
     pass_send, pass_recv, right_in, energy_in) = scratch[parts * energies + 2 :]
    me_e = lax.axis_index("energy")
    me_s = lax.axis_index("slab")
    has_left, has_right = me_s > 0, me_s < n_slab - 1
    odd = lax.rem(me_e, 2)
    to_far = me_e - 1 + 2 * odd
    to_near = me_e + 1 - 2 * odd
    has_far = (to_far >= 0) & (to_far < n_energy)
    has_near = (to_near >= 0) & (to_near < n_energy)

    def energy_of(step):
        return step + odd * (energies - 1 - 2 * step)

    last, late = parts - 1, 0
    handed = (late, WID - 1)
    orders = [list(range(energies)) for _ in range(parts)]
    orders[last] = [i for i in range(energies) if i != late] + [late]
    gives = (has_far, has_far & (odd == 0))
    takes = (has_far, has_far & (odd == 1))

    def far_units(r):
        return [u for u in range(WID) if r != last or u != late]

    small = [
        pltpu.make_async_copy(src, dst, small_sem.at[k])
        for k, (src, dst) in enumerate(((nbr_hbm, nbr), (shifts_hbm, shifts), (occ_hbm, occ)))
    ]
    has_prev, has_next = me_e > 0, me_e < n_energy - 1
    barrier = pltpu.get_barrier_semaphore()

    def tell(there, sem, device):
        @pl.when(there)
        def _():
            pl.semaphore_signal(sem, inc=1, device_id=device, device_id_type=MESH)

    tell(has_right, barrier, {"slab": me_s + 1})
    uneven = lax.rem(me_e, 2)
    energy_peers = has_prev.astype(jnp.int32) + has_next.astype(jnp.int32)
    for there, device in ((has_prev, {"energy": me_e - 1}), (has_next, {"energy": me_e + 1})):
        tell(there & (uneven == 1), barrier, device)
    for copy in small:
        copy.start()
    coup_copy = pltpu.make_async_copy(coupling, coup, coup_sem)
    local = [
        [
            pltpu.make_async_copy(green.at[energy_of(i), :, r], wide[r][i].at[HALO : HALO + atoms], local_sem.at[r, i])
            for i in range(energies)
        ]
        for r in range(parts)
    ]
    local[0][0].start()
    coup_copy.start()
    for r in range(parts):
        for i in range(energies):
            if r or i:
                local[r][i].start()

    entered = has_left.astype(jnp.int32) + (1 - uneven) * energy_peers

    @pl.when(entered > 0)
    def _():
        pl.semaphore_wait(barrier, entered)

    tell(has_left, right_in, {"slab": me_s - 1})
    for there, device in ((has_prev, {"energy": me_e - 1}), (has_next, {"energy": me_e + 1})):
        tell(there & (uneven == 0), energy_in, device)

    def slab_copy(r, i, direction):
        halo, e = wide[r][i], energy_of(i)
        if direction == 0:
            src, dst, to = green.at[e, atoms - HALO : atoms, r], halo.at[0:HALO], me_s + 1
        else:
            src, dst, to = green.at[e, 0:HALO, r], halo.at[HALO + atoms : 2 * HALO + atoms], me_s - 1
        return pltpu.make_async_remote_copy(
            src_ref=src,
            dst_ref=dst,
            send_sem=slab_send.at[direction, r, i],
            recv_sem=slab_recv.at[direction, r, i],
            device_id={"slab": to},
            device_id_type=MESH,
        )

    def raw_copy(k):
        return pltpu.make_async_remote_copy(
            src_ref=green.at[energy_of(handed[k]), :, last],
            dst_ref=foreign[k].at[HALO : HALO + atoms],
            send_sem=raw_send.at[k],
            recv_sem=raw_recv.at[k],
            device_id={"energy": to_far},
            device_id_type=MESH,
        )

    def pass_copy(k, direction):
        halo = foreign[k]
        if direction == 0:
            src, dst, to = halo.at[atoms : HALO + atoms], halo.at[0:HALO], me_s + 1
        else:
            src, dst, to = halo.at[HALO : 2 * HALO], halo.at[HALO + atoms : 2 * HALO + atoms], me_s - 1
        return pltpu.make_async_remote_copy(
            src_ref=src,
            dst_ref=dst,
            send_sem=pass_send.at[k, direction],
            recv_sem=pass_recv.at[k, direction],
            device_id={"slab": to},
            device_id_type=MESH,
        )

    @pl.when(has_left)
    def _():
        for r in range(parts):
            for i in orders[r]:
                slab_copy(r, i, 1).start()
    @pl.when(has_right)
    def _():
        pl.semaphore_wait(right_in, 1)
        for r in range(parts):
            for i in orders[r]:
                slab_copy(r, i, 0).start()

    @pl.when(uneven * energy_peers > 0)
    def _():
        pl.semaphore_wait(energy_in, energy_peers)

    for k in range(2):
        @pl.when(gives[k])
        def _(k=k):
            raw_copy(k).start()

    def energy_copy(r, u, direction):
        if direction == 0:
            src, dst, to = far_send.at[r, u], far_recv.at[r, u], to_far
        else:
            src, dst, to = near_send.at[r, u], near_recv.at[r, u], to_near
        return pltpu.make_async_remote_copy(
            src_ref=src,
            dst_ref=dst,
            send_sem=en_send.at[direction, r, u],
            recv_sem=en_recv.at[direction, r, u],
            device_id={"energy": to},
            device_id_type=MESH,
        )

    @pl.when(jnp.logical_not(has_far))
    def _():
        far_recv[...] = jnp.zeros_like(far_recv)
    @pl.when(jnp.logical_not(has_near))
    def _():
        near_recv[...] = jnp.zeros_like(near_recv)

    first_atom = me_s * atoms

    def products(source, store):
        halves, mats = [], []
        for a in range(atoms):
            mats.append([coup[a, j] for j in range(slots)])
            halves.append([])
            for j in range(slots):
                g = source[jnp.clip(nbr[a, j] - first_atom + HALO, 0, atoms + 2 * HALO - 1)]
                h = jnp.dot(mats[a][j].reshape(modes * blk, blk), g, preferred_element_type=jnp.float32)
                halves[a].append(h.astype(jnp.bfloat16))
        for a in range(atoms):
            for m in range(modes):
                lhs = jnp.concatenate([h[m * blk : (m + 1) * blk] for h in halves[a]], axis=1)
                rhs = jnp.concatenate([c[m] for c in mats[a]], axis=1)
                p = lax.dot_general(lhs, rhs, (((1,), (1,)), ((), ())), preferred_element_type=jnp.float32)
                store(m, a, p.astype(jnp.bfloat16))

    def store_sum(target, r, u, terms, spare=0, but=()):
        def body(a, carry):
            total = None
            for m, index, weight in terms:
                inside = (index >= 0) & (index < energies)
                for step in but:
                    inside = inside & (index != step)
                safe = jnp.where(inside, index, spare)
                term = jnp.where(inside, weight, 0.0) * prod[m, r, safe, a].astype(jnp.float32)
                total = term if total is None else total + term
            target[r, u, a] = total.astype(target.dtype)
            return carry

        lax.fori_loop(0, atoms, body, 0)

    odd_f = odd.astype(jnp.float32)

    def toward_far(m):
        return occ[m] + odd_f

    def toward_near(m):
        return occ[m] + (1.0 - odd_f)

    def own_sums(r, but=()):
        for t in range(energies):
            terms = []
            for m in range(modes):
                terms.append((m, t - shifts[m], toward_near(m)))
                terms.append((m, t + shifts[m], toward_far(m)))
            store_sum(own, r, t, terms, orders[r][0], but)

    def finish(r, t):
        far_u = WID - 1 - t if WID - 1 - t in far_units(r) else None
        near_u = energies - 1 - t if t >= energies - WID else None
        if near_u is not None:
            @pl.when(has_near)
            def _():
                energy_copy(r, near_u, 1).wait_recv()
        if far_u is not None:
            @pl.when(has_far)
            def _():
                energy_copy(r, far_u, 0).wait_recv()
        e = energy_of(t)

        def body(a, carry):
            total = own[r, t, a]
            if far_u is not None:
                total = total + far_recv[r, far_u, a].astype(jnp.float32)
            if near_u is not None:
                total = total + near_recv[r, near_u, a].astype(jnp.float32)
            if r == last:
                for m in range(modes):
                    if t != late and abs(t - late) <= WID:
                        weight = jnp.where(shifts[m] == abs(t - late), toward_near(m) if t > late else toward_far(m), 0.0)
                        total = total + weight * prod[m, r, late, a].astype(jnp.float32)
                    for k, step in enumerate(handed):
                        if t + 1 + step <= WID:
                            weight = jnp.where(shifts[m] == t + 1 + step, toward_near(m), 0.0)
                            total = total + weight * prod_f[k, m, a].astype(jnp.float32)
            out[e, a, r] = total.astype(jnp.bfloat16)
            return carry

        lax.fori_loop(0, atoms, body, 0)

    for r in range(parts):
        done, sent = set(), set()
        for i in orders[r]:
            if r == last and i == late:
                own_sums(r, (late,))
            local[r][i].wait()
            if r == 0 and not done:
                coup_copy.wait()
                for copy in small:
                    copy.wait()
            @pl.when(has_left)
            def _(i=i, r=r):
                slab_copy(r, i, 0).wait_recv()
            @pl.when(has_right)
            def _(i=i, r=r):
                slab_copy(r, i, 1).wait_recv()

            def store(m, a, value, r=r, i=i):
                prod[m, r, i, a] = value

            products(wide[r][i], store)
            done.add(i)
            for side in range(2):
                for u in far_units(r):
                    but = handed[: 2 - side] if r == last else ()
                    needed = {k for k in range(u - WID + 1, u + 1) if k >= 0 and k not in but}
                    if (side, u) in sent or not needed <= done:
                        continue
                    sent.add((side, u))
                    @pl.when(has_far & (odd == side))
                    def _(u=u, r=r, but=but):
                        terms = [(m, u - WID + shifts[m], toward_far(m)) for m in range(modes)]
                        store_sum(far_send, r, u, terms, orders[r][0], but)
                        energy_copy(r, u, 0).start()
            if r == 0 and len(done) == 3:
                for k in range(2):
                    @pl.when(takes[k])
                    def _(k=k):
                        raw_copy(k).wait_recv()
                        @pl.when(has_right)
                        def _():
                            pass_copy(k, 0).start()
                        @pl.when(has_left)
                        def _():
                            pass_copy(k, 1).start()
        for u in range(WID):
            @pl.when(has_near)
            def _(u=u, r=r):
                store_sum(near_send, r, u, [(m, energies + u - shifts[m], toward_near(m)) for m in range(modes)])
                energy_copy(r, u, 1).start()
        if r < last:
            own_sums(r)

    for r in range(last):
        for t in reversed(range(energies)):
            finish(r, t)

    for k in range(2):
        @pl.when(takes[k])
        def _(k=k):
            @pl.when(has_left)
            def _():
                pass_copy(k, 0).wait_recv()
            @pl.when(has_right)
            def _():
                pass_copy(k, 1).wait_recv()

            def store(m, a, value):
                prod_f[k, m, a] = value

            products(foreign[k], store)

        @pl.when(jnp.logical_not(takes[k]))
        def _(k=k):
            prod_f[k] = jnp.zeros_like(prod_f[k])

    for t in reversed(range(energies)):
        finish(last, t)

    for k in range(2):
        @pl.when(gives[k])
        def _(k=k):
            raw_copy(k).wait_send()
        @pl.when(takes[k] & has_right)
        def _(k=k):
            pass_copy(k, 0).wait_send()
        @pl.when(takes[k] & has_left)
        def _(k=k):
            pass_copy(k, 1).wait_send()

    for r in range(parts):
        for i in range(energies):
            @pl.when(has_right)
            def _(i=i, r=r):
                slab_copy(r, i, 0).wait_send()
            @pl.when(has_left)
            def _(i=i, r=r):
                slab_copy(r, i, 1).wait_send()
        for u in far_units(r):
            @pl.when(has_far)
            def _(u=u, r=r):
                energy_copy(r, u, 0).wait_send()
        for u in range(WID):
            @pl.when(has_near)
            def _(u=u, r=r):
                energy_copy(r, u, 1).wait_send()


def solution(mesh):
    def shards(green, coupling, neighbours, shifts, occupation):
        energies, atoms, parts, blk, _ = green.shape
        slots, modes = coupling.shape[1:3]
        sizes = (energies, atoms, parts, blk, slots, modes, mesh.shape["energy"], mesh.shape["slab"])
        bf16, f32 = jnp.bfloat16, jnp.float32
        hbm = pl.BlockSpec(memory_space=pltpu.HBM)
        edge = (parts, WID, atoms, blk, blk)
        dma = pltpu.SemaphoreType.DMA
        return pl.pallas_call(
            functools.partial(kernel, sizes),
            out_shape=pltpu.VMEM(green.shape, bf16),
            in_specs=[hbm] * 5,
            out_specs=pl.BlockSpec(memory_space=pltpu.VMEM),
            scratch_shapes=[pltpu.VMEM((atoms + 2 * HALO, blk, blk), bf16) for _ in range(parts * energies + 2)]
            + [
                pltpu.VMEM(coupling.shape, bf16),
                pltpu.VMEM((modes, parts, energies, atoms, blk, blk), bf16),
                pltpu.VMEM(edge, bf16),
                pltpu.VMEM(edge, bf16),
                pltpu.VMEM(edge, bf16),
                pltpu.VMEM(edge, bf16),
                pltpu.VMEM((parts, energies, atoms, blk, blk), f32),
                pltpu.SMEM((atoms, slots), jnp.int32),
                pltpu.SMEM((modes,), jnp.int32),
                pltpu.SMEM((modes,), f32),
                dma,
                dma((parts, energies)),
                dma((2, parts, energies)),
                dma((2, parts, energies)),
                dma((2, parts, WID)),
                dma((2, parts, WID)),
                dma((3,)),
                pltpu.VMEM((2, modes, atoms, blk, blk), bf16),
                dma((2,)),
                dma((2,)),
                dma((2, 2)),
                dma((2, 2)),
                pltpu.SemaphoreType.REGULAR,
                pltpu.SemaphoreType.REGULAR,
            ],
            compiler_params=pltpu.CompilerParams(collective_id=0, has_side_effects=True),
        )(neighbours, shifts, occupation, green, coupling)

    return jax.shard_map(
        shards,
        mesh=mesh,
        in_specs=(
            P("energy", "slab", None, None, None),
            P("slab", None, None, None, None),
            P("slab", None),
            P(),
            P(),
        ),
        out_specs=P("energy", "slab", None, None, None),
        check_vma=False,
    )
```

```python
import functools

import jax
import jax.numpy as jnp
from jax import lax
from jax.experimental import pallas as pl
from jax.experimental.pallas import tpu as pltpu
from jax.sharding import PartitionSpec as P

WID = 4
HALO = 2
MESH = pl.DeviceIdType.MESH


def kernel(sizes, nbr_hbm, shifts_hbm, occ_hbm, green, coupling, out, *scratch):
    energies, atoms, parts, blk, slots, modes, n_energy, n_slab = sizes
    wide = [scratch[r * energies : (r + 1) * energies] for r in range(parts)]
    foreign = scratch[parts * energies : parts * energies + 2]
    (coup, prod, near_send, far_send, near_recv, far_recv, own, nbr, shifts, occ,
     coup_sem, local_sem, slab_send, slab_recv, en_send, en_recv, small_sem, prod_f, raw_send, raw_recv,
     pass_send, pass_recv, right_in, energy_in) = scratch[parts * energies + 2 :]
    me_e = lax.axis_index("energy")
    me_s = lax.axis_index("slab")
    has_left, has_right = me_s > 0, me_s < n_slab - 1
    odd = lax.rem(me_e, 2)
    to_far = me_e - 1 + 2 * odd
    to_near = me_e + 1 - 2 * odd
    has_far = (to_far >= 0) & (to_far < n_energy)
    has_near = (to_near >= 0) & (to_near < n_energy)

    def energy_of(step):
        return step + odd * (energies - 1 - 2 * step)

    last, late = parts - 1, 0
    handed = (late, WID - 2)
    rising = list(range(energies))
    orders = [[rising] * last + [[i for i in rising if i not in held] + held[::-1]] for held in (list(handed), [late])]

    def step_at(r, p):
        even_step, odd_step = orders[0][r][p], orders[1][r][p]
        return even_step if even_step == odd_step else even_step + odd * (odd_step - even_step)

    gives = (has_far, has_far & (odd == 0))
    takes = (has_far, has_far & (odd == 1))

    def far_units(r):
        return [u for u in range(WID) if r != last or u != late]

    small = [
        pltpu.make_async_copy(src, dst, small_sem.at[k])
        for k, (src, dst) in enumerate(((nbr_hbm, nbr), (shifts_hbm, shifts), (occ_hbm, occ)))
    ]
    has_prev, has_next = me_e > 0, me_e < n_energy - 1
    barrier = pltpu.get_barrier_semaphore()

    def tell(there, sem, device):
        @pl.when(there)
        def _():
            pl.semaphore_signal(sem, inc=1, device_id=device, device_id_type=MESH)

    tell(has_right, barrier, {"slab": me_s + 1})
    uneven = lax.rem(me_e, 2)
    energy_peers = has_prev.astype(jnp.int32) + has_next.astype(jnp.int32)
    for there, device in ((has_prev, {"energy": me_e - 1}), (has_next, {"energy": me_e + 1})):
        tell(there & (uneven == 1), barrier, device)
    coup_copy = pltpu.make_async_copy(coupling, coup, coup_sem)
    local = [
        [
            pltpu.make_async_copy(green.at[energy_of(step_at(r, i)), :, r], wide[r][i].at[HALO : HALO + atoms], local_sem.at[r, i])
            for i in range(energies)
        ]
        for r in range(parts)
    ]

    entered = has_left.astype(jnp.int32) + (1 - uneven) * energy_peers

    @pl.when(entered > 0)
    def _():
        pl.semaphore_wait(barrier, entered)

    tell(has_left, right_in, {"slab": me_s - 1})
    for there, device in ((has_prev, {"energy": me_e - 1}), (has_next, {"energy": me_e + 1})):
        tell(there & (uneven == 0), energy_in, device)

    def slab_copy(r, i, direction):
        halo, e = wide[r][i], energy_of(step_at(r, i))
        if direction == 0:
            src, dst, to = green.at[e, atoms - HALO : atoms, r], halo.at[0:HALO], me_s + 1
        else:
            src, dst, to = green.at[e, 0:HALO, r], halo.at[HALO + atoms : 2 * HALO + atoms], me_s - 1
        return pltpu.make_async_remote_copy(
            src_ref=src,
            dst_ref=dst,
            send_sem=slab_send.at[direction, r, i],
            recv_sem=slab_recv.at[direction, r, i],
            device_id={"slab": to},
            device_id_type=MESH,
        )

    def raw_copy(k):
        return pltpu.make_async_remote_copy(
            src_ref=green.at[energy_of(handed[k]), :, last],
            dst_ref=foreign[k].at[HALO : HALO + atoms],
            send_sem=raw_send.at[k],
            recv_sem=raw_recv.at[k],
            device_id={"energy": to_far},
            device_id_type=MESH,
        )

    def pass_copy(k, direction):
        halo = foreign[k]
        if direction == 0:
            src, dst, to = halo.at[atoms : HALO + atoms], halo.at[0:HALO], me_s + 1
        else:
            src, dst, to = halo.at[HALO : 2 * HALO], halo.at[HALO + atoms : 2 * HALO + atoms], me_s - 1
        return pltpu.make_async_remote_copy(
            src_ref=src,
            dst_ref=dst,
            send_sem=pass_send.at[k, direction],
            recv_sem=pass_recv.at[k, direction],
            device_id={"slab": to},
            device_id_type=MESH,
        )

    @pl.when(has_left)
    def _():
        for r in range(parts):
            for i in range(energies):
                slab_copy(r, i, 1).start()
    for copy in small:
        copy.start()
    coup_copy.start()
    for r in range(parts):
        for i in range(energies):
            local[r][i].start()
    @pl.when(has_right)
    def _():
        pl.semaphore_wait(right_in, 1)
        for r in range(parts):
            for i in range(energies):
                slab_copy(r, i, 0).start()

    @pl.when(uneven * energy_peers > 0)
    def _():
        pl.semaphore_wait(energy_in, energy_peers)

    for k in range(2):
        @pl.when(gives[k])
        def _(k=k):
            raw_copy(k).start()

    def energy_copy(r, u, direction):
        if direction == 0:
            src, dst, to = far_send.at[r, u], far_recv.at[r, u], to_far
        else:
            src, dst, to = near_send.at[r, u], near_recv.at[r, u], to_near
        return pltpu.make_async_remote_copy(
            src_ref=src,
            dst_ref=dst,
            send_sem=en_send.at[direction, r, u],
            recv_sem=en_recv.at[direction, r, u],
            device_id={"energy": to},
            device_id_type=MESH,
        )

    @pl.when(jnp.logical_not(has_far))
    def _():
        far_recv[...] = jnp.zeros_like(far_recv)
    @pl.when(jnp.logical_not(has_near))
    def _():
        near_recv[...] = jnp.zeros_like(near_recv)

    first_atom = me_s * atoms

    def products(source, store):
        halves, mats = [], []
        for a in range(atoms):
            mats.append([coup[a, j] for j in range(slots)])
            halves.append([])
            for j in range(slots):
                g = source[jnp.clip(nbr[a, j] - first_atom + HALO, 0, atoms + 2 * HALO - 1)]
                h = jnp.dot(mats[a][j].reshape(modes * blk, blk), g, preferred_element_type=jnp.float32)
                halves[a].append(h.astype(jnp.bfloat16))
        for a in range(atoms):
            for m in range(modes):
                lhs = jnp.concatenate([h[m * blk : (m + 1) * blk] for h in halves[a]], axis=1)
                rhs = jnp.concatenate([c[m] for c in mats[a]], axis=1)
                p = lax.dot_general(lhs, rhs, (((1,), (1,)), ((), ())), preferred_element_type=jnp.float32)
                store(m, a, p.astype(jnp.bfloat16))

    def store_sum(target, r, u, terms, spare=0, but=()):
        def body(a, carry):
            total = None
            for m, index, weight in terms:
                inside = (index >= 0) & (index < energies)
                for step in but:
                    inside = inside & (index != step)
                safe = jnp.where(inside, index, spare)
                term = jnp.where(inside, weight, 0.0) * prod[m, r, safe, a].astype(jnp.float32)
                total = term if total is None else total + term
            target[r, u, a] = total.astype(target.dtype)
            return carry

        lax.fori_loop(0, atoms, body, 0)

    odd_f = odd.astype(jnp.float32)

    def toward_far(m):
        return occ[m] + odd_f

    def toward_near(m):
        return occ[m] + (1.0 - odd_f)

    def own_sums(r, but=()):
        for t in range(energies):
            terms = []
            for m in range(modes):
                terms.append((m, t - shifts[m], toward_near(m)))
                terms.append((m, t + shifts[m], toward_far(m)))
            store_sum(own, r, t, terms, orders[0][r][0], but)

    def finish(r, t):
        far_u = WID - 1 - t if WID - 1 - t in far_units(r) else None
        near_u = energies - 1 - t if t >= energies - WID else None
        if near_u is not None:
            @pl.when(has_near)
            def _():
                energy_copy(r, near_u, 1).wait_recv()
        if far_u is not None:
            @pl.when(has_far)
            def _():
                energy_copy(r, far_u, 0).wait_recv()
        e = energy_of(t)

        def body(a, carry):
            total = own[r, t, a]
            if far_u is not None:
                total = total + far_recv[r, far_u, a].astype(jnp.float32)
            if near_u is not None:
                total = total + near_recv[r, near_u, a].astype(jnp.float32)
            if r == last:
                for m in range(modes):
                    if t != late and abs(t - late) <= WID:
                        weight = jnp.where(shifts[m] == abs(t - late), toward_near(m) if t > late else toward_far(m), 0.0)
                        total = total + weight * prod[m, r, late, a].astype(jnp.float32)
                    for k, step in enumerate(handed):
                        if t + 1 + step <= WID:
                            weight = jnp.where(shifts[m] == t + 1 + step, toward_near(m), 0.0)
                            total = total + weight * prod_f[k, m, a].astype(jnp.float32)
            out[e, a, r] = total.astype(jnp.bfloat16)
            return carry

        lax.fori_loop(0, atoms, body, 0)

    for r in range(parts):
        sent = set()
        for i in range(energies):
            if r == last and i == energies - 1:
                own_sums(r, (late,))
            local[r][i].wait()
            if r == 0 and i == 0:
                coup_copy.wait()
                for copy in small:
                    copy.wait()
            @pl.when(has_left)
            def _(i=i, r=r):
                slab_copy(r, i, 0).wait_recv()
            @pl.when(has_right)
            def _(i=i, r=r):
                slab_copy(r, i, 1).wait_recv()

            def store(m, a, value, r=r, i=i):
                prod[m, r, step_at(r, i), a] = value

            products(wide[r][i], store)
            for side in range(2):
                done = set(orders[side][r][: i + 1])
                for u in far_units(r):
                    but = handed[: 2 - side] if r == last else ()
                    needed = {k for k in range(u - WID + 1, u + 1) if k >= 0 and k not in but}
                    if (side, u) in sent or not needed <= done:
                        continue
                    sent.add((side, u))
                    @pl.when(has_far & (odd == side))
                    def _(u=u, r=r, but=but):
                        terms = [(m, u - WID + shifts[m], toward_far(m)) for m in range(modes)]
                        store_sum(far_send, r, u, terms, orders[0][r][0], but)
                        energy_copy(r, u, 0).start()
            done = set(orders[0][r][: i + 1]) & set(orders[1][r][: i + 1])
            for u in reversed(range(WID)):
                needed = set(range(energies - WID + u, energies))
                if ("near", u) in sent or not (needed <= done or i == energies - 1):
                    continue
                sent.add(("near", u))
                @pl.when(has_near)
                def _(u=u, r=r):
                    terms = [(m, energies + u - shifts[m], toward_near(m)) for m in range(modes)]
                    store_sum(near_send, r, u, terms, orders[0][r][0])
                    energy_copy(r, u, 1).start()
            if r == 0 and i == 2:
                for k in range(2):
                    @pl.when(takes[k])
                    def _(k=k):
                        raw_copy(k).wait_recv()
                        @pl.when(has_right)
                        def _():
                            pass_copy(k, 0).start()
                        @pl.when(has_left)
                        def _():
                            pass_copy(k, 1).start()
        if r < last:
            own_sums(r)

    for r in range(last):
        for t in reversed(range(energies)):
            finish(r, t)

    for k in range(2):
        @pl.when(gives[k])
        def _(k=k):
            raw_copy(k).wait_send()
    @pl.when(has_far)
    def _():
        for r in range(last):
            for u in far_units(r):
                energy_copy(r, u, 0).wait_send()
    @pl.when(has_near)
    def _():
        for r in range(last):
            for u in range(WID):
                energy_copy(r, u, 1).wait_send()
    @pl.when(has_left)
    def _():
        for r in range(parts):
            for i in range(energies):
                slab_copy(r, i, 1).wait_send()
    @pl.when(has_right)
    def _():
        for r in range(parts):
            for i in range(energies):
                slab_copy(r, i, 0).wait_send()

    for k in range(2):
        @pl.when(takes[k])
        def _(k=k):
            @pl.when(has_left)
            def _():
                pass_copy(k, 0).wait_recv()
            @pl.when(has_right)
            def _():
                pass_copy(k, 1).wait_recv()

            def store(m, a, value):
                prod_f[k, m, a] = value

            products(foreign[k], store)

        @pl.when(jnp.logical_not(takes[k]))
        def _(k=k):
            prod_f[k] = jnp.zeros_like(prod_f[k])

    for t in reversed(range(energies)):
        finish(last, t)

    @pl.when(has_far)
    def _():
        for u in far_units(last):
            energy_copy(last, u, 0).wait_send()
    @pl.when(has_near)
    def _():
        for u in range(WID):
            energy_copy(last, u, 1).wait_send()
    for k in range(2):
        @pl.when(takes[k] & has_right)
        def _(k=k):
            pass_copy(k, 0).wait_send()
        @pl.when(takes[k] & has_left)
        def _(k=k):
            pass_copy(k, 1).wait_send()


def solution(mesh):
    def shards(green, coupling, neighbours, shifts, occupation):
        energies, atoms, parts, blk, _ = green.shape
        slots, modes = coupling.shape[1:3]
        sizes = (energies, atoms, parts, blk, slots, modes, mesh.shape["energy"], mesh.shape["slab"])
        bf16, f32 = jnp.bfloat16, jnp.float32
        hbm = pl.BlockSpec(memory_space=pltpu.HBM)
        edge = (parts, WID, atoms, blk, blk)
        dma = pltpu.SemaphoreType.DMA
        return pl.pallas_call(
            functools.partial(kernel, sizes),
            out_shape=pltpu.VMEM(green.shape, bf16),
            in_specs=[hbm] * 5,
            out_specs=pl.BlockSpec(memory_space=pltpu.VMEM),
            scratch_shapes=[pltpu.VMEM((atoms + 2 * HALO, blk, blk), bf16) for _ in range(parts * energies + 2)]
            + [
                pltpu.VMEM(coupling.shape, bf16),
                pltpu.VMEM((modes, parts, energies, atoms, blk, blk), bf16),
                pltpu.VMEM(edge, bf16),
                pltpu.VMEM(edge, bf16),
                pltpu.VMEM(edge, bf16),
                pltpu.VMEM(edge, bf16),
                pltpu.VMEM((parts, energies, atoms, blk, blk), f32),
                pltpu.SMEM((atoms, slots), jnp.int32),
                pltpu.SMEM((modes,), jnp.int32),
                pltpu.SMEM((modes,), f32),
                dma,
                dma((parts, energies)),
                dma((2, parts, energies)),
                dma((2, parts, energies)),
                dma((2, parts, WID)),
                dma((2, parts, WID)),
                dma((3,)),
                pltpu.VMEM((2, modes, atoms, blk, blk), bf16),
                dma((2,)),
                dma((2,)),
                dma((2, 2)),
                dma((2, 2)),
                pltpu.SemaphoreType.REGULAR,
                pltpu.SemaphoreType.REGULAR,
            ],
            compiler_params=pltpu.CompilerParams(collective_id=0, has_side_effects=True),
        )(neighbours, shifts, occupation, green, coupling)

    return jax.shard_map(
        shards,
        mesh=mesh,
        in_specs=(
            P("energy", "slab", None, None, None),
            P("slab", None, None, None, None),
            P("slab", None),
            P(),
            P(),
        ),
        out_specs=P("energy", "slab", None, None, None),
        check_vma=False,
    )
```

```python
import functools

import jax
import jax.numpy as jnp
from jax import lax
from jax.experimental import pallas as pl
from jax.experimental.pallas import tpu as pltpu
from jax.sharding import PartitionSpec as P

WID = 4
HALO = 2
MESH = pl.DeviceIdType.MESH


def kernel(sizes, nbr_hbm, shifts_hbm, occ_hbm, green, coupling, out, *scratch):
    energies, atoms, parts, blk, slots, modes, n_energy, n_slab = sizes
    wide = [scratch[r * energies : (r + 1) * energies] for r in range(parts)]
    foreign = scratch[parts * energies : parts * energies + 2]
    (coup, prod, near_send, far_send, near_recv, far_recv, own, nbr, shifts, occ,
     coup_sem, local_sem, slab_send, slab_recv, en_send, en_recv, small_sem, prod_f, raw_send, raw_recv,
     pass_send, pass_recv, right_in, energy_in) = scratch[parts * energies + 2 :]
    me_e = lax.axis_index("energy")
    me_s = lax.axis_index("slab")
    has_left, has_right = me_s > 0, me_s < n_slab - 1
    odd = lax.rem(me_e, 2)
    to_far = me_e - 1 + 2 * odd
    to_near = me_e + 1 - 2 * odd
    has_far = (to_far >= 0) & (to_far < n_energy)
    has_near = (to_near >= 0) & (to_near < n_energy)

    def energy_of(step):
        return step + odd * (energies - 1 - 2 * step)

    last, late = parts - 1, 0
    handed = (late, WID - 2)
    rising = list(range(energies))
    orders = [[rising] * last + [[i for i in rising if i not in held] + held[::-1]] for held in (list(handed), [late])]

    def step_at(r, p):
        even_step, odd_step = orders[0][r][p], orders[1][r][p]
        return even_step if even_step == odd_step else even_step + odd * (odd_step - even_step)

    gives = (has_far, has_far & (odd == 0))
    takes = (has_far, has_far & (odd == 1))

    def far_units(r):
        return [u for u in range(WID) if r != last or u != late]

    small = [
        pltpu.make_async_copy(src, dst, small_sem.at[k])
        for k, (src, dst) in enumerate(((nbr_hbm, nbr), (shifts_hbm, shifts), (occ_hbm, occ)))
    ]
    has_prev, has_next = me_e > 0, me_e < n_energy - 1
    barrier = pltpu.get_barrier_semaphore()

    def tell(there, sem, device):
        @pl.when(there)
        def _():
            pl.semaphore_signal(sem, inc=1, device_id=device, device_id_type=MESH)

    tell(has_right, barrier, {"slab": me_s + 1})
    uneven = lax.rem(me_e, 2)
    energy_peers = has_prev.astype(jnp.int32) + has_next.astype(jnp.int32)
    for there, device in ((has_prev, {"energy": me_e - 1}), (has_next, {"energy": me_e + 1})):
        tell(there & (uneven == 1), barrier, device)
    coup_copy = pltpu.make_async_copy(coupling, coup, coup_sem)
    local = [
        [
            pltpu.make_async_copy(green.at[energy_of(step_at(r, i)), :, r], wide[r][i].at[HALO : HALO + atoms], local_sem.at[r, i])
            for i in range(energies)
        ]
        for r in range(parts)
    ]

    entered = has_left.astype(jnp.int32) + (1 - uneven) * energy_peers

    @pl.when(entered > 0)
    def _():
        pl.semaphore_wait(barrier, entered)

    tell(has_left, right_in, {"slab": me_s - 1})
    for there, device in ((has_prev, {"energy": me_e - 1}), (has_next, {"energy": me_e + 1})):
        tell(there & (uneven == 0), energy_in, device)

    def slab_copy(r, i, direction):
        halo, e = wide[r][i], energy_of(step_at(r, i))
        if direction == 0:
            src, dst, to = green.at[e, atoms - HALO : atoms, r], halo.at[0:HALO], me_s + 1
        else:
            src, dst, to = green.at[e, 0:HALO, r], halo.at[HALO + atoms : 2 * HALO + atoms], me_s - 1
        return pltpu.make_async_remote_copy(
            src_ref=src,
            dst_ref=dst,
            send_sem=slab_send.at[direction, r, i],
            recv_sem=slab_recv.at[direction, r, i],
            device_id={"slab": to},
            device_id_type=MESH,
        )

    def raw_copy(k):
        return pltpu.make_async_remote_copy(
            src_ref=green.at[energy_of(handed[k]), :, last],
            dst_ref=foreign[k].at[HALO : HALO + atoms],
            send_sem=raw_send.at[k],
            recv_sem=raw_recv.at[k],
            device_id={"energy": to_far},
            device_id_type=MESH,
        )

    def pass_copy(k, direction):
        halo = foreign[k]
        if direction == 0:
            src, dst, to = halo.at[atoms : HALO + atoms], halo.at[0:HALO], me_s + 1
        else:
            src, dst, to = halo.at[HALO : 2 * HALO], halo.at[HALO + atoms : 2 * HALO + atoms], me_s - 1
        return pltpu.make_async_remote_copy(
            src_ref=src,
            dst_ref=dst,
            send_sem=pass_send.at[k, direction],
            recv_sem=pass_recv.at[k, direction],
            device_id={"slab": to},
            device_id_type=MESH,
        )

    @pl.when(has_left)
    def _():
        for r in range(parts):
            for i in range(energies):
                slab_copy(r, i, 1).start()
    for copy in small:
        copy.start()
    coup_copy.start()
    for r in range(parts):
        for i in range(energies):
            local[r][i].start()
    @pl.when(has_right)
    def _():
        pl.semaphore_wait(right_in, 1)
        for r in range(parts):
            for i in range(energies):
                slab_copy(r, i, 0).start()

    @pl.when(uneven * energy_peers > 0)
    def _():
        pl.semaphore_wait(energy_in, energy_peers)

    for k in range(2):
        @pl.when(gives[k])
        def _(k=k):
            raw_copy(k).start()

    def energy_copy(r, u, direction):
        if direction == 0:
            src, dst, to = far_send.at[r, u], far_recv.at[r, u], to_far
        else:
            src, dst, to = near_send.at[r, u], near_recv.at[r, u], to_near
        return pltpu.make_async_remote_copy(
            src_ref=src,
            dst_ref=dst,
            send_sem=en_send.at[direction, r, u],
            recv_sem=en_recv.at[direction, r, u],
            device_id={"energy": to},
            device_id_type=MESH,
        )

    @pl.when(jnp.logical_not(has_far))
    def _():
        far_recv[...] = jnp.zeros_like(far_recv)
    @pl.when(jnp.logical_not(has_near))
    def _():
        near_recv[...] = jnp.zeros_like(near_recv)

    first_atom = me_s * atoms

    def mode(q):
        widest = sum(m * (shifts[m] == WID).astype(jnp.int32) for m in range(modes))
        return widest if q == 0 else q - 1 + (widest <= q - 1).astype(jnp.int32)

    def shift(q):
        return WID if q == 0 else shifts[mode(q)]

    every = list(range(modes))

    def products(source, store, roles):
        halves, mats = [], []
        for a in range(atoms):
            mats.append([jnp.concatenate([coup[a, j, mode(q)] for q in roles], axis=0) for j in range(slots)])
            halves.append([])
            for j in range(slots):
                g = source[jnp.clip(nbr[a, j] - first_atom + HALO, 0, atoms + 2 * HALO - 1)]
                h = jnp.dot(mats[a][j], g, preferred_element_type=jnp.float32)
                halves[a].append(h.astype(jnp.bfloat16))
        for a in range(atoms):
            for k, q in enumerate(roles):
                lhs = jnp.concatenate([h[k * blk : (k + 1) * blk] for h in halves[a]], axis=1)
                rhs = jnp.concatenate([c[k * blk : (k + 1) * blk] for c in mats[a]], axis=1)
                p = lax.dot_general(lhs, rhs, (((1,), (1,)), ((), ())), preferred_element_type=jnp.float32)
                store(q, a, p.astype(jnp.bfloat16))

    def store_sum(target, r, u, terms, spare=0, but=()):
        def body(a, carry):
            total = None
            for m, index, weight in terms:
                if isinstance(index, int):
                    if not 0 <= index < energies or index in but:
                        continue
                    term = weight * prod[m, r, index, a].astype(jnp.float32)
                else:
                    inside = (index >= 0) & (index < energies)
                    for step in but:
                        inside = inside & (index != step)
                    safe = jnp.where(inside, index, spare)
                    term = jnp.where(inside, weight, 0.0) * prod[m, r, safe, a].astype(jnp.float32)
                total = term if total is None else total + term
            target[r, u, a] = total.astype(target.dtype)
            return carry

        lax.fori_loop(0, atoms, body, 0)

    odd_f = odd.astype(jnp.float32)

    def toward_far(m):
        return occ[mode(m)] + odd_f

    def toward_near(m):
        return occ[mode(m)] + (1.0 - odd_f)

    def own_sums(r, but=()):
        for t in range(energies):
            terms = []
            for m in range(modes):
                terms.append((m, t - shift(m), toward_near(m)))
                terms.append((m, t + shift(m), toward_far(m)))
            store_sum(own, r, t, terms, orders[0][r][0], but)

    def finish(r, t):
        far_u = WID - 1 - t if WID - 1 - t in far_units(r) else None
        near_u = energies - 1 - t if t >= energies - WID else None
        if near_u is not None:
            @pl.when(has_near)
            def _():
                energy_copy(r, near_u, 1).wait_recv()
        if far_u is not None:
            @pl.when(has_far)
            def _():
                energy_copy(r, far_u, 0).wait_recv()
        e = energy_of(t)

        def body(a, carry):
            total = own[r, t, a]
            if far_u is not None:
                total = total + far_recv[r, far_u, a].astype(jnp.float32)
            if near_u is not None:
                total = total + near_recv[r, near_u, a].astype(jnp.float32)
            if r == last:
                def add(total, distance, weight, value):
                    if distance == WID:
                        return total + weight(0) * value(0).astype(jnp.float32)
                    for q in every[1:] if distance < WID else []:
                        total = total + jnp.where(shift(q) == distance, weight(q), 0.0) * value(q).astype(jnp.float32)
                    return total

                if t != late:
                    side = toward_near if t > late else toward_far
                    total = add(total, abs(t - late), side, lambda q: prod[q, r, late, a])
                for k, step in enumerate(handed):
                    total = add(total, t + 1 + step, toward_near, lambda q: prod_f[k, q, a])
            out[e, a, r] = total.astype(jnp.bfloat16)
            return carry

        lax.fori_loop(0, atoms, body, 0)

    for r in range(parts):
        sent = set()
        for i in range(energies):
            if r == last and i == energies - 1:
                own_sums(r, (late,))
            local[r][i].wait()
            if r == 0 and i == 0:
                coup_copy.wait()
                for copy in small:
                    copy.wait()
            @pl.when(has_left)
            def _(i=i, r=r):
                slab_copy(r, i, 0).wait_recv()
            @pl.when(has_right)
            def _(i=i, r=r):
                slab_copy(r, i, 1).wait_recv()

            def store(m, a, value, r=r, i=i):
                prod[m, r, step_at(r, i), a] = value

            products(wide[r][i], store, every)
            for side in range(2):
                done = set(orders[side][r][: i + 1])
                but = handed[: 2 - side] if r == last else ()
                for u in far_units(r):
                    wide_step = {u} - set(but)
                    others = {k for k in range(u - WID + 1, u) if k >= 0 and k not in but}
                    if (side, u) in sent or not wide_step | others <= done:
                        continue
                    sent.add((side, u))
                    @pl.when(has_far & (odd == side))
                    def _(u=u, r=r, but=but, others=others):
                        terms = [(q, u - WID + shift(q), toward_far(q)) for q in (every if others else every[:1])]
                        store_sum(far_send, r, u, terms, min(others, default=u), but)
                        energy_copy(r, u, 0).start()
                for u in reversed(range(WID)):
                    others = set(range(energies - WID + u + 1, energies))
                    if ("near", side, u) in sent or not {energies - WID + u} | others <= done:
                        continue
                    sent.add(("near", side, u))
                    @pl.when(has_near & (odd == side))
                    def _(u=u, r=r, others=others):
                        terms = [(q, energies + u - shift(q), toward_near(q)) for q in (every if others else every[:1])]
                        store_sum(near_send, r, u, terms, min(others, default=u))
                        energy_copy(r, u, 1).start()
            if r == 0 and i == 2:
                for k in range(2):
                    @pl.when(takes[k])
                    def _(k=k):
                        raw_copy(k).wait_recv()
                        @pl.when(has_right)
                        def _():
                            pass_copy(k, 0).start()
                        @pl.when(has_left)
                        def _():
                            pass_copy(k, 1).start()
        if r < last:
            own_sums(r)

    for r in range(last):
        for t in reversed(range(energies)):
            finish(r, t)

    for k in range(2):
        @pl.when(gives[k])
        def _(k=k):
            raw_copy(k).wait_send()
    @pl.when(has_far)
    def _():
        for r in range(last):
            for u in far_units(r):
                energy_copy(r, u, 0).wait_send()
    @pl.when(has_near)
    def _():
        for r in range(last):
            for u in range(WID):
                energy_copy(r, u, 1).wait_send()
    @pl.when(has_left)
    def _():
        for r in range(parts):
            for i in range(energies):
                slab_copy(r, i, 1).wait_send()
    @pl.when(has_right)
    def _():
        for r in range(parts):
            for i in range(energies):
                slab_copy(r, i, 0).wait_send()

    for k in range(2):
        @pl.when(takes[k])
        def _(k=k):
            @pl.when(has_left)
            def _():
                pass_copy(k, 0).wait_recv()
            @pl.when(has_right)
            def _():
                pass_copy(k, 1).wait_recv()

            def store(m, a, value):
                prod_f[k, m, a] = value

            products(foreign[k], store, every)

        @pl.when(jnp.logical_not(takes[k]))
        def _(k=k):
            prod_f[k] = jnp.zeros_like(prod_f[k])

    for t in reversed(range(energies)):
        finish(last, t)

    @pl.when(has_far)
    def _():
        for u in far_units(last):
            energy_copy(last, u, 0).wait_send()
    @pl.when(has_near)
    def _():
        for u in range(WID):
            energy_copy(last, u, 1).wait_send()
    for k in range(2):
        @pl.when(takes[k] & has_right)
        def _(k=k):
            pass_copy(k, 0).wait_send()
        @pl.when(takes[k] & has_left)
        def _(k=k):
            pass_copy(k, 1).wait_send()


def solution(mesh):
    def shards(green, coupling, neighbours, shifts, occupation):
        energies, atoms, parts, blk, _ = green.shape
        slots, modes = coupling.shape[1:3]
        sizes = (energies, atoms, parts, blk, slots, modes, mesh.shape["energy"], mesh.shape["slab"])
        bf16, f32 = jnp.bfloat16, jnp.float32
        hbm = pl.BlockSpec(memory_space=pltpu.HBM)
        edge = (parts, WID, atoms, blk, blk)
        dma = pltpu.SemaphoreType.DMA
        return pl.pallas_call(
            functools.partial(kernel, sizes),
            out_shape=pltpu.VMEM(green.shape, bf16),
            in_specs=[hbm] * 5,
            out_specs=pl.BlockSpec(memory_space=pltpu.VMEM),
            scratch_shapes=[pltpu.VMEM((atoms + 2 * HALO, blk, blk), bf16) for _ in range(parts * energies + 2)]
            + [
                pltpu.VMEM(coupling.shape, bf16),
                pltpu.VMEM((modes, parts, energies, atoms, blk, blk), bf16),
                pltpu.VMEM(edge, bf16),
                pltpu.VMEM(edge, bf16),
                pltpu.VMEM(edge, bf16),
                pltpu.VMEM(edge, bf16),
                pltpu.VMEM((parts, energies, atoms, blk, blk), f32),
                pltpu.SMEM((atoms, slots), jnp.int32),
                pltpu.SMEM((modes,), jnp.int32),
                pltpu.SMEM((modes,), f32),
                dma,
                dma((parts, energies)),
                dma((2, parts, energies)),
                dma((2, parts, energies)),
                dma((2, parts, WID)),
                dma((2, parts, WID)),
                dma((3,)),
                pltpu.VMEM((2, modes, atoms, blk, blk), bf16),
                dma((2,)),
                dma((2,)),
                dma((2, 2)),
                dma((2, 2)),
                pltpu.SemaphoreType.REGULAR,
                pltpu.SemaphoreType.REGULAR,
            ],
            compiler_params=pltpu.CompilerParams(collective_id=0, has_side_effects=True),
        )(neighbours, shifts, occupation, green, coupling)

    return jax.shard_map(
        shards,
        mesh=mesh,
        in_specs=(
            P("energy", "slab", None, None, None),
            P("slab", None, None, None, None),
            P("slab", None),
            P(),
            P(),
        ),
        out_specs=P("energy", "slab", None, None, None),
        check_vma=False,
    )
```

```python
import functools

import jax
import jax.numpy as jnp
from jax import lax
from jax.experimental import pallas as pl
from jax.experimental.pallas import tpu as pltpu
from jax.sharding import PartitionSpec as P

WID = 4
HALO = 2
MESH = pl.DeviceIdType.MESH


def kernel(sizes, nbr_hbm, shifts_hbm, occ_hbm, green, coupling, out, *scratch):
    energies, atoms, parts, blk, slots, modes, n_energy, n_slab = sizes
    wide = [scratch[r * energies : (r + 1) * energies] for r in range(parts)]
    foreign = scratch[parts * energies : parts * energies + 2]
    (coup, prod, near_send, far_send, near_recv, far_recv, own, nbr, shifts, occ,
     coup_sem, local_sem, slab_send, slab_recv, en_send, en_recv, small_sem, prod_f, raw_send, raw_recv,
     pass_send, pass_recv, right_in, energy_in) = scratch[parts * energies + 2 :]
    me_e = lax.axis_index("energy")
    me_s = lax.axis_index("slab")
    has_left, has_right = me_s > 0, me_s < n_slab - 1
    odd = lax.rem(me_e, 2)
    to_far = me_e - 1 + 2 * odd
    to_near = me_e + 1 - 2 * odd
    has_far = (to_far >= 0) & (to_far < n_energy)
    has_near = (to_near >= 0) & (to_near < n_energy)

    def energy_of(step):
        return step + odd * (energies - 1 - 2 * step)

    last, late = parts - 1, 0
    handed = (late, WID - 2)
    rising = list(range(energies))
    orders = [[rising] * last + [[i for i in rising if i not in held] + held[::-1]] for held in (list(handed), [late])]

    def step_at(r, p):
        even_step, odd_step = orders[0][r][p], orders[1][r][p]
        return even_step if even_step == odd_step else even_step + odd * (odd_step - even_step)

    gives = (has_far, has_far & (odd == 0))
    takes = (has_far, has_far & (odd == 1))

    def far_units(r):
        return [u for u in range(WID) if r != last or u != late]

    small = [
        pltpu.make_async_copy(src, dst, small_sem.at[k])
        for k, (src, dst) in enumerate(((nbr_hbm, nbr), (shifts_hbm, shifts), (occ_hbm, occ)))
    ]
    has_prev, has_next = me_e > 0, me_e < n_energy - 1
    barrier = pltpu.get_barrier_semaphore()

    def tell(there, sem, device):
        @pl.when(there)
        def _():
            pl.semaphore_signal(sem, inc=1, device_id=device, device_id_type=MESH)

    tell(has_right, barrier, {"slab": me_s + 1})
    uneven = lax.rem(me_e, 2)
    energy_peers = has_prev.astype(jnp.int32) + has_next.astype(jnp.int32)
    for there, device in ((has_prev, {"energy": me_e - 1}), (has_next, {"energy": me_e + 1})):
        tell(there & (uneven == 1), barrier, device)
    coup_copy = pltpu.make_async_copy(coupling, coup, coup_sem)
    local = [
        [
            pltpu.make_async_copy(green.at[energy_of(step_at(r, i)), :, r], wide[r][i].at[HALO : HALO + atoms], local_sem.at[r, i])
            for i in range(energies)
        ]
        for r in range(parts)
    ]

    entered = has_left.astype(jnp.int32) + (1 - uneven) * energy_peers

    @pl.when(entered > 0)
    def _():
        pl.semaphore_wait(barrier, entered)

    tell(has_left, right_in, {"slab": me_s - 1})
    for there, device in ((has_prev, {"energy": me_e - 1}), (has_next, {"energy": me_e + 1})):
        tell(there & (uneven == 0), energy_in, device)

    def slab_copy(r, i, direction):
        halo, e = wide[r][i], energy_of(step_at(r, i))
        if direction == 0:
            src, dst, to = green.at[e, atoms - HALO : atoms, r], halo.at[0:HALO], me_s + 1
            if r or i:
                src = halo.at[atoms : HALO + atoms]
        else:
            src, dst, to = green.at[e, 0:HALO, r], halo.at[HALO + atoms : 2 * HALO + atoms], me_s - 1
            if r or i:
                src = halo.at[HALO : 2 * HALO]
        return pltpu.make_async_remote_copy(
            src_ref=src,
            dst_ref=dst,
            send_sem=slab_send.at[direction, r, i],
            recv_sem=slab_recv.at[direction, r, i],
            device_id={"slab": to},
            device_id_type=MESH,
        )

    def raw_copy(k):
        return pltpu.make_async_remote_copy(
            src_ref=green.at[energy_of(handed[k]), :, last],
            dst_ref=foreign[k].at[HALO : HALO + atoms],
            send_sem=raw_send.at[k],
            recv_sem=raw_recv.at[k],
            device_id={"energy": to_far},
            device_id_type=MESH,
        )

    def pass_copy(k, direction):
        halo = foreign[k]
        if direction == 0:
            src, dst, to = halo.at[atoms : HALO + atoms], halo.at[0:HALO], me_s + 1
        else:
            src, dst, to = halo.at[HALO : 2 * HALO], halo.at[HALO + atoms : 2 * HALO + atoms], me_s - 1
        return pltpu.make_async_remote_copy(
            src_ref=src,
            dst_ref=dst,
            send_sem=pass_send.at[k, direction],
            recv_sem=pass_recv.at[k, direction],
            device_id={"slab": to},
            device_id_type=MESH,
        )

    @pl.when(has_left)
    def _():
        slab_copy(0, 0, 1).start()
    for r in range(parts):
        for i in range(energies):
            local[r][i].start()
    for copy in small:
        copy.start()
    coup_copy.start()
    for r in range(parts):
        for i in range(energies):
            local[r][i].wait()
            if r or i:
                @pl.when(has_left)
                def _(r=r, i=i):
                    slab_copy(r, i, 1).start()
    @pl.when(has_right)
    def _():
        pl.semaphore_wait(right_in, 1)
        for r in range(parts):
            for i in range(energies):
                slab_copy(r, i, 0).start()

    @pl.when(uneven * energy_peers > 0)
    def _():
        pl.semaphore_wait(energy_in, energy_peers)

    for k in range(2):
        @pl.when(gives[k])
        def _(k=k):
            raw_copy(k).start()

    def energy_copy(r, u, direction):
        if direction == 0:
            src, dst, to = far_send.at[r, u], far_recv.at[r, u], to_far
        else:
            src, dst, to = near_send.at[r, u], near_recv.at[r, u], to_near
        return pltpu.make_async_remote_copy(
            src_ref=src,
            dst_ref=dst,
            send_sem=en_send.at[direction, r, u],
            recv_sem=en_recv.at[direction, r, u],
            device_id={"energy": to},
            device_id_type=MESH,
        )

    @pl.when(jnp.logical_not(has_far))
    def _():
        far_recv[...] = jnp.zeros_like(far_recv)
    @pl.when(jnp.logical_not(has_near))
    def _():
        near_recv[...] = jnp.zeros_like(near_recv)

    first_atom = me_s * atoms

    def mode(q):
        widest = sum(m * (shifts[m] == WID).astype(jnp.int32) for m in range(modes))
        return widest if q == 0 else q - 1 + (widest <= q - 1).astype(jnp.int32)

    def shift(q):
        return WID if q == 0 else shifts[mode(q)]

    every = list(range(modes))

    def products(source, store, roles):
        halves, mats = [], []
        for a in range(atoms):
            mats.append([jnp.concatenate([coup[a, j, mode(q)] for q in roles], axis=0) for j in range(slots)])
            halves.append([])
            for j in range(slots):
                g = source[jnp.clip(nbr[a, j] - first_atom + HALO, 0, atoms + 2 * HALO - 1)]
                h = jnp.dot(mats[a][j], g, preferred_element_type=jnp.float32)
                halves[a].append(h.astype(jnp.bfloat16))
        for a in range(atoms):
            for k, q in enumerate(roles):
                lhs = jnp.concatenate([h[k * blk : (k + 1) * blk] for h in halves[a]], axis=1)
                rhs = jnp.concatenate([c[k * blk : (k + 1) * blk] for c in mats[a]], axis=1)
                p = lax.dot_general(lhs, rhs, (((1,), (1,)), ((), ())), preferred_element_type=jnp.float32)
                store(q, a, p.astype(jnp.bfloat16))

    def store_sum(target, r, u, terms, spare=0, but=()):
        def body(a, carry):
            total = None
            for m, index, weight in terms:
                if isinstance(index, int):
                    if not 0 <= index < energies or index in but:
                        continue
                    term = weight * prod[m, r, index, a].astype(jnp.float32)
                else:
                    inside = (index >= 0) & (index < energies)
                    for step in but:
                        inside = inside & (index != step)
                    safe = jnp.where(inside, index, spare)
                    term = jnp.where(inside, weight, 0.0) * prod[m, r, safe, a].astype(jnp.float32)
                total = term if total is None else total + term
            target[r, u, a] = total.astype(target.dtype)
            return carry

        lax.fori_loop(0, atoms, body, 0)

    odd_f = odd.astype(jnp.float32)

    def toward_far(m):
        return occ[mode(m)] + odd_f

    def toward_near(m):
        return occ[mode(m)] + (1.0 - odd_f)

    def own_sums(r, but=()):
        for t in range(energies):
            terms = []
            for m in range(modes):
                terms.append((m, t - shift(m), toward_near(m)))
                terms.append((m, t + shift(m), toward_far(m)))
            store_sum(own, r, t, terms, orders[0][r][0], but)

    def finish(r, t):
        far_u = WID - 1 - t if WID - 1 - t in far_units(r) else None
        near_u = energies - 1 - t if t >= energies - WID else None
        if near_u is not None:
            @pl.when(has_near)
            def _():
                energy_copy(r, near_u, 1).wait_recv()
        if far_u is not None:
            @pl.when(has_far)
            def _():
                energy_copy(r, far_u, 0).wait_recv()
        e = energy_of(t)

        def body(a, carry):
            total = own[r, t, a]
            if far_u is not None:
                total = total + far_recv[r, far_u, a].astype(jnp.float32)
            if near_u is not None:
                total = total + near_recv[r, near_u, a].astype(jnp.float32)
            if r == last:
                def add(total, distance, weight, value):
                    if distance == WID:
                        return total + weight(0) * value(0).astype(jnp.float32)
                    for q in every[1:] if distance < WID else []:
                        total = total + jnp.where(shift(q) == distance, weight(q), 0.0) * value(q).astype(jnp.float32)
                    return total

                if t != late:
                    side = toward_near if t > late else toward_far
                    total = add(total, abs(t - late), side, lambda q: prod[q, r, late, a])
                for k, step in enumerate(handed):
                    total = add(total, t + 1 + step, toward_near, lambda q: prod_f[k, q, a])
            out[e, a, r] = total.astype(jnp.bfloat16)
            return carry

        lax.fori_loop(0, atoms, body, 0)

    for r in range(parts):
        sent = set()
        for i in range(energies):
            if r == last and i == energies - 1:
                own_sums(r, (late,))
            if r == 0 and i == 0:
                coup_copy.wait()
                for copy in small:
                    copy.wait()
            @pl.when(has_left)
            def _(i=i, r=r):
                slab_copy(r, i, 0).wait_recv()
            @pl.when(has_right)
            def _(i=i, r=r):
                slab_copy(r, i, 1).wait_recv()

            def store(m, a, value, r=r, i=i):
                prod[m, r, step_at(r, i), a] = value

            products(wide[r][i], store, every)
            for side in range(2):
                done = set(orders[side][r][: i + 1])
                but = handed[: 2 - side] if r == last else ()
                for u in far_units(r):
                    wide_step = {u} - set(but)
                    others = {k for k in range(u - WID + 1, u) if k >= 0 and k not in but}
                    if (side, u) in sent or not wide_step | others <= done:
                        continue
                    sent.add((side, u))
                    @pl.when(has_far & (odd == side))
                    def _(u=u, r=r, but=but, others=others):
                        terms = [(q, u - WID + shift(q), toward_far(q)) for q in (every if others else every[:1])]
                        store_sum(far_send, r, u, terms, min(others, default=u), but)
                        energy_copy(r, u, 0).start()
                for u in reversed(range(WID)):
                    others = set(range(energies - WID + u + 1, energies))
                    if ("near", side, u) in sent or not {energies - WID + u} | others <= done:
                        continue
                    sent.add(("near", side, u))
                    @pl.when(has_near & (odd == side))
                    def _(u=u, r=r, others=others):
                        terms = [(q, energies + u - shift(q), toward_near(q)) for q in (every if others else every[:1])]
                        store_sum(near_send, r, u, terms, min(others, default=u))
                        energy_copy(r, u, 1).start()
            if r == 0 and i == 2:
                for k in range(2):
                    @pl.when(takes[k])
                    def _(k=k):
                        raw_copy(k).wait_recv()
                        @pl.when(has_right)
                        def _():
                            pass_copy(k, 0).start()
                        @pl.when(has_left)
                        def _():
                            pass_copy(k, 1).start()
        if r < last:
            own_sums(r)

    for r in range(last):
        for t in reversed(range(energies)):
            finish(r, t)

    for k in range(2):
        @pl.when(gives[k])
        def _(k=k):
            raw_copy(k).wait_send()
    @pl.when(has_far)
    def _():
        for r in range(last):
            for u in far_units(r):
                energy_copy(r, u, 0).wait_send()
    @pl.when(has_near)
    def _():
        for r in range(last):
            for u in range(WID):
                energy_copy(r, u, 1).wait_send()
    @pl.when(has_left)
    def _():
        for r in range(parts):
            for i in range(energies):
                slab_copy(r, i, 1).wait_send()
    @pl.when(has_right)
    def _():
        for r in range(parts):
            for i in range(energies):
                slab_copy(r, i, 0).wait_send()

    for k in range(2):
        @pl.when(takes[k])
        def _(k=k):
            @pl.when(has_left)
            def _():
                pass_copy(k, 0).wait_recv()
            @pl.when(has_right)
            def _():
                pass_copy(k, 1).wait_recv()

            def store(m, a, value):
                prod_f[k, m, a] = value

            products(foreign[k], store, every)

        @pl.when(jnp.logical_not(takes[k]))
        def _(k=k):
            prod_f[k] = jnp.zeros_like(prod_f[k])

    for t in reversed(range(energies)):
        finish(last, t)

    @pl.when(has_far)
    def _():
        for u in far_units(last):
            energy_copy(last, u, 0).wait_send()
    @pl.when(has_near)
    def _():
        for u in range(WID):
            energy_copy(last, u, 1).wait_send()
    for k in range(2):
        @pl.when(takes[k] & has_right)
        def _(k=k):
            pass_copy(k, 0).wait_send()
        @pl.when(takes[k] & has_left)
        def _(k=k):
            pass_copy(k, 1).wait_send()


def solution(mesh):
    def shards(green, coupling, neighbours, shifts, occupation):
        energies, atoms, parts, blk, _ = green.shape
        slots, modes = coupling.shape[1:3]
        sizes = (energies, atoms, parts, blk, slots, modes, mesh.shape["energy"], mesh.shape["slab"])
        bf16, f32 = jnp.bfloat16, jnp.float32
        hbm = pl.BlockSpec(memory_space=pltpu.HBM)
        edge = (parts, WID, atoms, blk, blk)
        dma = pltpu.SemaphoreType.DMA
        return pl.pallas_call(
            functools.partial(kernel, sizes),
            out_shape=pltpu.VMEM(green.shape, bf16),
            in_specs=[hbm] * 5,
            out_specs=pl.BlockSpec(memory_space=pltpu.VMEM),
            scratch_shapes=[pltpu.VMEM((atoms + 2 * HALO, blk, blk), bf16) for _ in range(parts * energies + 2)]
            + [
                pltpu.VMEM(coupling.shape, bf16),
                pltpu.VMEM((modes, parts, energies, atoms, blk, blk), bf16),
                pltpu.VMEM(edge, bf16),
                pltpu.VMEM(edge, bf16),
                pltpu.VMEM(edge, bf16),
                pltpu.VMEM(edge, bf16),
                pltpu.VMEM((parts, energies, atoms, blk, blk), f32),
                pltpu.SMEM((atoms, slots), jnp.int32),
                pltpu.SMEM((modes,), jnp.int32),
                pltpu.SMEM((modes,), f32),
                dma,
                dma((parts, energies)),
                dma((2, parts, energies)),
                dma((2, parts, energies)),
                dma((2, parts, WID)),
                dma((2, parts, WID)),
                dma((3,)),
                pltpu.VMEM((2, modes, atoms, blk, blk), bf16),
                dma((2,)),
                dma((2,)),
                dma((2, 2)),
                dma((2, 2)),
                pltpu.SemaphoreType.REGULAR,
                pltpu.SemaphoreType.REGULAR,
            ],
            compiler_params=pltpu.CompilerParams(collective_id=0, has_side_effects=True),
        )(neighbours, shifts, occupation, green, coupling)

    return jax.shard_map(
        shards,
        mesh=mesh,
        in_specs=(
            P("energy", "slab", None, None, None),
            P("slab", None, None, None, None),
            P("slab", None),
            P(),
            P(),
        ),
        out_specs=P("energy", "slab", None, None, None),
        check_vma=False,
    )
```

```python
import functools

import jax
import jax.numpy as jnp
from jax import lax
from jax.experimental import pallas as pl
from jax.experimental.pallas import tpu as pltpu
from jax.sharding import PartitionSpec as P

WID = 4
HALO = 2
MESH = pl.DeviceIdType.MESH


def kernel(sizes, nbr_hbm, shifts_hbm, occ_hbm, green, coupling, out, *scratch):
    energies, atoms, parts, blk, slots, modes, n_energy, n_slab = sizes
    wide = [scratch[r * energies : (r + 1) * energies] for r in range(parts)]
    foreign = scratch[parts * energies : parts * energies + 2]
    (coup, prod, near_send, far_send, near_recv, far_recv, own, nbr, shifts, occ,
     coup_sem, local_sem, slab_send, slab_recv, en_send, en_recv, small_sem, prod_f, raw_send, raw_recv,
     pass_send, pass_recv, right_in, energy_in) = scratch[parts * energies + 2 :]
    me_e = lax.axis_index("energy")
    me_s = lax.axis_index("slab")
    has_left, has_right = me_s > 0, me_s < n_slab - 1
    odd = lax.rem(me_e, 2)
    to_far = me_e - 1 + 2 * odd
    to_near = me_e + 1 - 2 * odd
    has_far = (to_far >= 0) & (to_far < n_energy)
    has_near = (to_near >= 0) & (to_near < n_energy)

    def energy_of(step):
        return step + odd * (energies - 1 - 2 * step)

    last, late = parts - 1, 0
    handed = (late, WID - 2)
    rising = list(range(energies))
    orders = [[rising] * last + [[i for i in rising if i not in held] + held[::-1]] for held in (list(handed), [late])]

    def step_at(r, p):
        even_step, odd_step = orders[0][r][p], orders[1][r][p]
        return even_step if even_step == odd_step else even_step + odd * (odd_step - even_step)

    gives = (has_far, has_far & (odd == 0))
    takes = (has_far, has_far & (odd == 1))

    def far_units(r):
        return [u for u in range(WID) if r != last or u != late]

    small = [
        pltpu.make_async_copy(src, dst, small_sem.at[k])
        for k, (src, dst) in enumerate(((nbr_hbm, nbr), (shifts_hbm, shifts), (occ_hbm, occ)))
    ]
    has_prev, has_next = me_e > 0, me_e < n_energy - 1
    barrier = pltpu.get_barrier_semaphore()

    def tell(there, sem, device):
        @pl.when(there)
        def _():
            pl.semaphore_signal(sem, inc=1, device_id=device, device_id_type=MESH)

    tell(has_right, barrier, {"slab": me_s + 1})
    uneven = lax.rem(me_e, 2)
    energy_peers = has_prev.astype(jnp.int32) + has_next.astype(jnp.int32)
    for there, device in ((has_prev, {"energy": me_e - 1}), (has_next, {"energy": me_e + 1})):
        tell(there & (uneven == 1), barrier, device)
    coup_copy = pltpu.make_async_copy(coupling, coup, coup_sem)
    local = [
        [
            pltpu.make_async_copy(green.at[energy_of(step_at(r, i)), :, r], wide[r][i].at[HALO : HALO + atoms], local_sem.at[r, i])
            for i in range(energies)
        ]
        for r in range(parts)
    ]

    entered = has_left.astype(jnp.int32) + (1 - uneven) * energy_peers

    @pl.when(entered > 0)
    def _():
        pl.semaphore_wait(barrier, entered)

    tell(has_left, right_in, {"slab": me_s - 1})
    for there, device in ((has_prev, {"energy": me_e - 1}), (has_next, {"energy": me_e + 1})):
        tell(there & (uneven == 0), energy_in, device)

    def slab_copy(r, i, direction):
        halo, e = wide[r][i], energy_of(step_at(r, i))
        if direction == 0:
            src, dst, to = green.at[e, atoms - HALO : atoms, r], halo.at[0:HALO], me_s + 1
            if r or i:
                src = halo.at[atoms : HALO + atoms]
        else:
            src, dst, to = green.at[e, 0:HALO, r], halo.at[HALO + atoms : 2 * HALO + atoms], me_s - 1
            if r or i:
                src = halo.at[HALO : 2 * HALO]
        return pltpu.make_async_remote_copy(
            src_ref=src,
            dst_ref=dst,
            send_sem=slab_send.at[direction, r, i],
            recv_sem=slab_recv.at[direction, r, i],
            device_id={"slab": to},
            device_id_type=MESH,
        )

    def raw_copy(k):
        return pltpu.make_async_remote_copy(
            src_ref=green.at[energy_of(handed[k]), :, last],
            dst_ref=foreign[k].at[HALO : HALO + atoms],
            send_sem=raw_send.at[k],
            recv_sem=raw_recv.at[k],
            device_id={"energy": to_far},
            device_id_type=MESH,
        )

    def pass_copy(k, direction):
        halo = foreign[k]
        if direction == 0:
            src, dst, to = halo.at[atoms : HALO + atoms], halo.at[0:HALO], me_s + 1
        else:
            src, dst, to = halo.at[HALO : 2 * HALO], halo.at[HALO + atoms : 2 * HALO + atoms], me_s - 1
        return pltpu.make_async_remote_copy(
            src_ref=src,
            dst_ref=dst,
            send_sem=pass_send.at[k, direction],
            recv_sem=pass_recv.at[k, direction],
            device_id={"slab": to},
            device_id_type=MESH,
        )

    @pl.when(has_left)
    def _():
        slab_copy(0, 0, 1).start()
    for r in range(parts):
        for i in range(energies):
            local[r][i].start()
    for copy in small:
        copy.start()
    coup_copy.start()
    for r in range(parts):
        for i in range(energies):
            local[r][i].wait()
            if r or i:
                @pl.when(has_left)
                def _(r=r, i=i):
                    slab_copy(r, i, 1).start()
    @pl.when(has_right)
    def _():
        pl.semaphore_wait(right_in, 1)
        for r in range(parts):
            for i in range(energies):
                slab_copy(r, i, 0).start()

    @pl.when(uneven * energy_peers > 0)
    def _():
        pl.semaphore_wait(energy_in, energy_peers)

    for k in range(2):
        @pl.when(gives[k])
        def _(k=k):
            raw_copy(k).start()

    def energy_copy(r, u, direction):
        if direction == 0:
            src, dst, to = far_send.at[r, u], far_recv.at[r, u], to_far
        else:
            src, dst, to = near_send.at[r, u], near_recv.at[r, u], to_near
        return pltpu.make_async_remote_copy(
            src_ref=src,
            dst_ref=dst,
            send_sem=en_send.at[direction, r, u],
            recv_sem=en_recv.at[direction, r, u],
            device_id={"energy": to},
            device_id_type=MESH,
        )

    @pl.when(jnp.logical_not(has_far))
    def _():
        far_recv[...] = jnp.zeros_like(far_recv)
    @pl.when(jnp.logical_not(has_near))
    def _():
        near_recv[...] = jnp.zeros_like(near_recv)

    first_atom = me_s * atoms

    def mode(q):
        widest = sum(m * (shifts[m] == WID).astype(jnp.int32) for m in range(modes))
        return widest if q == 0 else q - 1 + (widest <= q - 1).astype(jnp.int32)

    def shift(q):
        return WID if q == 0 else shifts[mode(q)]

    every = list(range(modes))

    def products(source, store, roles):
        halves, mats = [], []
        for a in range(atoms):
            mats.append([jnp.concatenate([coup[a, j, mode(q)] for q in roles], axis=0) for j in range(slots)])
            halves.append([])
            for j in range(slots):
                g = source[jnp.clip(nbr[a, j] - first_atom + HALO, 0, atoms + 2 * HALO - 1)]
                h = jnp.dot(mats[a][j], g, preferred_element_type=jnp.float32)
                halves[a].append(h.astype(jnp.bfloat16))
        for a in range(atoms):
            for k, q in enumerate(roles):
                lhs = jnp.concatenate([h[k * blk : (k + 1) * blk] for h in halves[a]], axis=1)
                rhs = jnp.concatenate([c[k * blk : (k + 1) * blk] for c in mats[a]], axis=1)
                p = lax.dot_general(lhs, rhs, (((1,), (1,)), ((), ())), preferred_element_type=jnp.float32)
                store(q, a, p.astype(jnp.bfloat16))

    def store_sum(target, r, u, terms, spare=0, but=()):
        def body(a, carry):
            total = None
            for m, index, weight in terms:
                if isinstance(index, int):
                    if not 0 <= index < energies or index in but:
                        continue
                    term = weight * prod[m, r, index, a].astype(jnp.float32)
                else:
                    inside = (index >= 0) & (index < energies)
                    for step in but:
                        inside = inside & (index != step)
                    safe = jnp.where(inside, index, spare)
                    term = jnp.where(inside, weight, 0.0) * prod[m, r, safe, a].astype(jnp.float32)
                total = term if total is None else total + term
            target[r, u, a] = total.astype(target.dtype)
            return carry

        lax.fori_loop(0, atoms, body, 0)

    odd_f = odd.astype(jnp.float32)

    def toward_far(m):
        return occ[mode(m)] + odd_f

    def toward_near(m):
        return occ[mode(m)] + (1.0 - odd_f)

    def own_sums(r, but=()):
        for t in range(energies):
            terms = []
            for m in range(modes):
                terms.append((m, t - shift(m), toward_near(m)))
                terms.append((m, t + shift(m), toward_far(m)))
            store_sum(own, r, t, terms, orders[0][r][0], but)

    def finish(r, t):
        far_u = WID - 1 - t if WID - 1 - t in far_units(r) else None
        near_u = energies - 1 - t if t >= energies - WID else None
        if near_u is not None:
            @pl.when(has_near)
            def _():
                energy_copy(r, near_u, 1).wait_recv()
        if far_u is not None:
            @pl.when(has_far)
            def _():
                energy_copy(r, far_u, 0).wait_recv()
        e = energy_of(t)

        def body(a, carry):
            total = own[r, t, a]
            if far_u is not None:
                total = total + far_recv[r, far_u, a].astype(jnp.float32)
            if near_u is not None:
                total = total + near_recv[r, near_u, a].astype(jnp.float32)
            if r == last:
                def add(total, distance, weight, value):
                    if distance == WID:
                        return total + weight(0) * value(0).astype(jnp.float32)
                    for q in every[1:] if distance < WID else []:
                        total = total + jnp.where(shift(q) == distance, weight(q), 0.0) * value(q).astype(jnp.float32)
                    return total

                if t != late:
                    side = toward_near if t > late else toward_far
                    total = add(total, abs(t - late), side, lambda q: prod[q, r, late, a])
                for k, step in enumerate(handed):
                    total = add(total, t + 1 + step, toward_near, lambda q: prod_f[k, q, a])
            out[e, a, r] = total.astype(jnp.bfloat16)
            return carry

        lax.fori_loop(0, atoms, body, 0)

    for r in range(parts):
        sent = set()
        for i in range(energies):
            if r == last and i == energies - 1:
                own_sums(r, (late,))
            if r == 0 and i == 0:
                coup_copy.wait()
                for copy in small:
                    copy.wait()
            @pl.when(has_left)
            def _(i=i, r=r):
                slab_copy(r, i, 0).wait_recv()
            @pl.when(has_right)
            def _(i=i, r=r):
                slab_copy(r, i, 1).wait_recv()

            def store(m, a, value, r=r, i=i):
                prod[m, r, step_at(r, i), a] = value

            products(wide[r][i], store, every)
            for side in range(2):
                done = set(orders[side][r][: i + 1])
                but = handed[: 2 - side] if r == last else ()
                for u in far_units(r):
                    wide_step = {u} - set(but)
                    others = {k for k in range(u - WID + 1, u) if k >= 0 and k not in but}
                    if (side, u) in sent or not wide_step | others <= done:
                        continue
                    sent.add((side, u))
                    @pl.when(has_far & (odd == side))
                    def _(u=u, r=r, but=but, others=others):
                        terms = [(q, u - WID + shift(q), toward_far(q)) for q in (every if others else every[:1])]
                        store_sum(far_send, r, u, terms, min(others, default=u), but)
                        energy_copy(r, u, 0).start()
                for u in reversed(range(WID)):
                    others = set(range(energies - WID + u + 1, energies))
                    if ("near", side, u) in sent or not {energies - WID + u} | others <= done:
                        continue
                    sent.add(("near", side, u))
                    @pl.when(has_near & (odd == side))
                    def _(u=u, r=r, others=others):
                        terms = [(q, energies + u - shift(q), toward_near(q)) for q in (every if others else every[:1])]
                        store_sum(near_send, r, u, terms, min(others, default=u))
                        energy_copy(r, u, 1).start()
            if r == 0 and i == 3:
                for k in range(2):
                    @pl.when(takes[k])
                    def _(k=k):
                        raw_copy(k).wait_recv()
                        @pl.when(has_right)
                        def _():
                            pass_copy(k, 0).start()
                        @pl.when(has_left)
                        def _():
                            pass_copy(k, 1).start()
        if r < last:
            own_sums(r)

    for r in range(last):
        for t in reversed(range(energies)):
            finish(r, t)

    for k in range(2):
        @pl.when(gives[k])
        def _(k=k):
            raw_copy(k).wait_send()
    @pl.when(has_far)
    def _():
        for r in range(last):
            for u in far_units(r):
                energy_copy(r, u, 0).wait_send()
    @pl.when(has_near)
    def _():
        for r in range(last):
            for u in range(WID):
                energy_copy(r, u, 1).wait_send()
    @pl.when(has_left)
    def _():
        for r in range(parts):
            for i in range(energies):
                slab_copy(r, i, 1).wait_send()
    @pl.when(has_right)
    def _():
        for r in range(parts):
            for i in range(energies):
                slab_copy(r, i, 0).wait_send()

    for k in range(2):
        @pl.when(takes[k])
        def _(k=k):
            @pl.when(has_left)
            def _():
                pass_copy(k, 0).wait_recv()
            @pl.when(has_right)
            def _():
                pass_copy(k, 1).wait_recv()

            def store(m, a, value):
                prod_f[k, m, a] = value

            products(foreign[k], store, every)

        @pl.when(jnp.logical_not(takes[k]))
        def _(k=k):
            prod_f[k] = jnp.zeros_like(prod_f[k])

    for t in reversed(range(energies)):
        finish(last, t)

    @pl.when(has_far)
    def _():
        for u in far_units(last):
            energy_copy(last, u, 0).wait_send()
    @pl.when(has_near)
    def _():
        for u in range(WID):
            energy_copy(last, u, 1).wait_send()
    for k in range(2):
        @pl.when(takes[k] & has_right)
        def _(k=k):
            pass_copy(k, 0).wait_send()
        @pl.when(takes[k] & has_left)
        def _(k=k):
            pass_copy(k, 1).wait_send()


def solution(mesh):
    def shards(green, coupling, neighbours, shifts, occupation):
        energies, atoms, parts, blk, _ = green.shape
        slots, modes = coupling.shape[1:3]
        sizes = (energies, atoms, parts, blk, slots, modes, mesh.shape["energy"], mesh.shape["slab"])
        bf16, f32 = jnp.bfloat16, jnp.float32
        hbm = pl.BlockSpec(memory_space=pltpu.HBM)
        edge = (parts, WID, atoms, blk, blk)
        dma = pltpu.SemaphoreType.DMA
        return pl.pallas_call(
            functools.partial(kernel, sizes),
            out_shape=pltpu.VMEM(green.shape, bf16),
            in_specs=[hbm] * 5,
            out_specs=pl.BlockSpec(memory_space=pltpu.VMEM),
            scratch_shapes=[pltpu.VMEM((atoms + 2 * HALO, blk, blk), bf16) for _ in range(parts * energies + 2)]
            + [
                pltpu.VMEM(coupling.shape, bf16),
                pltpu.VMEM((modes, parts, energies, atoms, blk, blk), bf16),
                pltpu.VMEM(edge, bf16),
                pltpu.VMEM(edge, bf16),
                pltpu.VMEM(edge, bf16),
                pltpu.VMEM(edge, bf16),
                pltpu.VMEM((parts, energies, atoms, blk, blk), f32),
                pltpu.SMEM((atoms, slots), jnp.int32),
                pltpu.SMEM((modes,), jnp.int32),
                pltpu.SMEM((modes,), f32),
                dma,
                dma((parts, energies)),
                dma((2, parts, energies)),
                dma((2, parts, energies)),
                dma((2, parts, WID)),
                dma((2, parts, WID)),
                dma((3,)),
                pltpu.VMEM((2, modes, atoms, blk, blk), bf16),
                dma((2,)),
                dma((2,)),
                dma((2, 2)),
                dma((2, 2)),
                pltpu.SemaphoreType.REGULAR,
                pltpu.SemaphoreType.REGULAR,
            ],
            compiler_params=pltpu.CompilerParams(collective_id=0, has_side_effects=True),
        )(neighbours, shifts, occupation, green, coupling)

    return jax.shard_map(
        shards,
        mesh=mesh,
        in_specs=(
            P("energy", "slab", None, None, None),
            P("slab", None, None, None, None),
            P("slab", None),
            P(),
            P(),
        ),
        out_specs=P("energy", "slab", None, None, None),
        check_vma=False,
    )
```

```python
import functools

import jax
import jax.numpy as jnp
from jax import lax
from jax.experimental import pallas as pl
from jax.experimental.pallas import tpu as pltpu
from jax.sharding import PartitionSpec as P

WID = 4
HALO = 2
MESH = pl.DeviceIdType.MESH


def kernel(sizes, nbr_hbm, shifts_hbm, occ_hbm, green, coupling, out, *scratch):
    energies, atoms, parts, blk, slots, modes, n_energy, n_slab = sizes
    wide = [scratch[r * energies : (r + 1) * energies] for r in range(parts)]
    foreign = scratch[parts * energies : parts * energies + 2]
    (coup, prod, near_send, far_send, near_recv, far_recv, own, nbr, shifts, occ,
     coup_sem, local_sem, slab_send, slab_recv, en_send, en_recv, small_sem, prod_f, raw_send, raw_recv,
     pass_send, pass_recv, right_in, energy_in) = scratch[parts * energies + 2 :]
    me_e = lax.axis_index("energy")
    me_s = lax.axis_index("slab")
    has_left, has_right = me_s > 0, me_s < n_slab - 1
    odd = lax.rem(me_e, 2)
    to_far = me_e - 1 + 2 * odd
    to_near = me_e + 1 - 2 * odd
    has_far = (to_far >= 0) & (to_far < n_energy)
    has_near = (to_near >= 0) & (to_near < n_energy)

    def energy_of(step):
        return step + odd * (energies - 1 - 2 * step)

    last, late = parts - 1, 0
    handed = (late, WID - 2)
    rising = list(range(energies))
    orders = [[rising] * last + [[i for i in rising if i not in held] + held[::-1]] for held in (list(handed), [late])]

    def step_at(r, p):
        even_step, odd_step = orders[0][r][p], orders[1][r][p]
        return even_step if even_step == odd_step else even_step + odd * (odd_step - even_step)

    gives = (has_far, has_far & (odd == 0))
    takes = (has_far, has_far & (odd == 1))

    def far_units(r):
        return [u for u in range(WID) if r != last or u != late]

    small = [
        pltpu.make_async_copy(src, dst, small_sem.at[k])
        for k, (src, dst) in enumerate(((nbr_hbm, nbr), (shifts_hbm, shifts), (occ_hbm, occ)))
    ]
    has_prev, has_next = me_e > 0, me_e < n_energy - 1
    barrier = pltpu.get_barrier_semaphore()

    def tell(there, sem, device):
        @pl.when(there)
        def _():
            pl.semaphore_signal(sem, inc=1, device_id=device, device_id_type=MESH)

    tell(has_right, barrier, {"slab": me_s + 1})
    uneven = lax.rem(me_e, 2)
    energy_peers = has_prev.astype(jnp.int32) + has_next.astype(jnp.int32)
    for there, device in ((has_prev, {"energy": me_e - 1}), (has_next, {"energy": me_e + 1})):
        tell(there & (uneven == 1), barrier, device)
    coup_copy = pltpu.make_async_copy(coupling, coup, coup_sem)
    local = [
        [
            pltpu.make_async_copy(green.at[energy_of(step_at(r, i)), :, r], wide[r][i].at[HALO : HALO + atoms], local_sem.at[r, i])
            for i in range(energies)
        ]
        for r in range(parts)
    ]

    entered = has_left.astype(jnp.int32) + (1 - uneven) * energy_peers

    @pl.when(entered > 0)
    def _():
        pl.semaphore_wait(barrier, entered)

    tell(has_left, right_in, {"slab": me_s - 1})
    for there, device in ((has_prev, {"energy": me_e - 1}), (has_next, {"energy": me_e + 1})):
        tell(there & (uneven == 0), energy_in, device)

    def slab_copy(r, i, direction):
        halo, e = wide[r][i], energy_of(step_at(r, i))
        if direction == 0:
            src, dst, to = green.at[e, atoms - HALO : atoms, r], halo.at[0:HALO], me_s + 1
            if r or i:
                src = halo.at[atoms : HALO + atoms]
        else:
            src, dst, to = green.at[e, 0:HALO, r], halo.at[HALO + atoms : 2 * HALO + atoms], me_s - 1
            if r or i:
                src = halo.at[HALO : 2 * HALO]
        return pltpu.make_async_remote_copy(
            src_ref=src,
            dst_ref=dst,
            send_sem=slab_send.at[direction, r, i],
            recv_sem=slab_recv.at[direction, r, i],
            device_id={"slab": to},
            device_id_type=MESH,
        )

    def raw_copy(k):
        return pltpu.make_async_remote_copy(
            src_ref=green.at[energy_of(handed[k]), :, last],
            dst_ref=foreign[k].at[HALO : HALO + atoms],
            send_sem=raw_send.at[k],
            recv_sem=raw_recv.at[k],
            device_id={"energy": to_far},
            device_id_type=MESH,
        )

    def pass_copy(k, direction):
        halo = foreign[k]
        if direction == 0:
            src, dst, to = halo.at[atoms : HALO + atoms], halo.at[0:HALO], me_s + 1
        else:
            src, dst, to = halo.at[HALO : 2 * HALO], halo.at[HALO + atoms : 2 * HALO + atoms], me_s - 1
        return pltpu.make_async_remote_copy(
            src_ref=src,
            dst_ref=dst,
            send_sem=pass_send.at[k, direction],
            recv_sem=pass_recv.at[k, direction],
            device_id={"slab": to},
            device_id_type=MESH,
        )

    @pl.when(has_left)
    def _():
        slab_copy(0, 0, 1).start()
    for r in range(parts):
        for i in range(energies):
            local[r][i].start()
    for copy in small:
        copy.start()
    coup_copy.start()
    for r in range(parts):
        for i in range(energies):
            local[r][i].wait()
            if r or i:
                @pl.when(has_left)
                def _(r=r, i=i):
                    slab_copy(r, i, 1).start()
    @pl.when(has_right)
    def _():
        pl.semaphore_wait(right_in, 1)
        for r in range(parts):
            for i in range(energies):
                slab_copy(r, i, 0).start()

    @pl.when(uneven * energy_peers > 0)
    def _():
        pl.semaphore_wait(energy_in, energy_peers)

    for k in range(2):
        @pl.when(gives[k])
        def _(k=k):
            raw_copy(k).start()

    def energy_copy(r, u, direction):
        if direction == 0:
            src, dst, to = far_send.at[r, u], far_recv.at[r, u], to_far
        else:
            src, dst, to = near_send.at[r, u], near_recv.at[r, u], to_near
        return pltpu.make_async_remote_copy(
            src_ref=src,
            dst_ref=dst,
            send_sem=en_send.at[direction, r, u],
            recv_sem=en_recv.at[direction, r, u],
            device_id={"energy": to},
            device_id_type=MESH,
        )

    @pl.when(jnp.logical_not(has_far))
    def _():
        far_recv[...] = jnp.zeros_like(far_recv)
    @pl.when(jnp.logical_not(has_near))
    def _():
        near_recv[...] = jnp.zeros_like(near_recv)

    first_atom = me_s * atoms

    def mode(q):
        widest = sum(m * (shifts[m] == WID).astype(jnp.int32) for m in range(modes))
        return widest if q == 0 else q - 1 + (widest <= q - 1).astype(jnp.int32)

    def shift(q):
        return WID if q == 0 else shifts[mode(q)]

    every = list(range(modes))

    def products(source, store, roles):
        halves, mats = [], []
        for a in range(atoms):
            mats.append([jnp.concatenate([coup[a, j, mode(q)] for q in roles], axis=0) for j in range(slots)])
            halves.append([])
            for j in range(slots):
                g = source[jnp.clip(nbr[a, j] - first_atom + HALO, 0, atoms + 2 * HALO - 1)]
                h = jnp.dot(mats[a][j], g, preferred_element_type=jnp.float32)
                halves[a].append(h.astype(jnp.bfloat16))
        for a in range(atoms):
            for k, q in enumerate(roles):
                lhs = jnp.concatenate([h[k * blk : (k + 1) * blk] for h in halves[a]], axis=1)
                rhs = jnp.concatenate([c[k * blk : (k + 1) * blk] for c in mats[a]], axis=1)
                p = lax.dot_general(lhs, rhs, (((1,), (1,)), ((), ())), preferred_element_type=jnp.float32)
                store(q, a, p.astype(jnp.bfloat16))

    def store_sum(target, r, u, terms, spare=0, but=()):
        def body(a, carry):
            total = None
            for m, index, weight in terms:
                if isinstance(index, int):
                    if not 0 <= index < energies or index in but:
                        continue
                    term = weight * prod[m, r, index, a].astype(jnp.float32)
                else:
                    inside = (index >= 0) & (index < energies)
                    for step in but:
                        inside = inside & (index != step)
                    safe = jnp.where(inside, index, spare)
                    term = jnp.where(inside, weight, 0.0) * prod[m, r, safe, a].astype(jnp.float32)
                total = term if total is None else total + term
            target[r, u, a] = total.astype(target.dtype)
            return carry

        lax.fori_loop(0, atoms, body, 0)

    odd_f = odd.astype(jnp.float32)

    def toward_far(m):
        return occ[mode(m)] + odd_f

    def toward_near(m):
        return occ[mode(m)] + (1.0 - odd_f)

    def own_sums(r, but=()):
        for t in range(energies):
            terms = []
            for m in range(modes):
                terms.append((m, t - shift(m), toward_near(m)))
                terms.append((m, t + shift(m), toward_far(m)))
            store_sum(own, r, t, terms, orders[0][r][0], but)

    def finish(r, t):
        far_u = WID - 1 - t if WID - 1 - t in far_units(r) else None
        near_u = energies - 1 - t if t >= energies - WID else None
        if near_u is not None:
            @pl.when(has_near)
            def _():
                energy_copy(r, near_u, 1).wait_recv()
        if far_u is not None:
            @pl.when(has_far)
            def _():
                energy_copy(r, far_u, 0).wait_recv()
        e = energy_of(t)

        def body(a, carry):
            total = own[r, t, a]
            if far_u is not None:
                total = total + far_recv[r, far_u, a].astype(jnp.float32)
            if near_u is not None:
                total = total + near_recv[r, near_u, a].astype(jnp.float32)
            if r == last:
                def add(total, distance, weight, value):
                    if distance == WID:
                        return total + weight(0) * value(0).astype(jnp.float32)
                    for q in every[1:] if distance < WID else []:
                        total = total + jnp.where(shift(q) == distance, weight(q), 0.0) * value(q).astype(jnp.float32)
                    return total

                if t != late:
                    side = toward_near if t > late else toward_far
                    total = add(total, abs(t - late), side, lambda q: prod[q, r, late, a])
                for k, step in enumerate(handed):
                    total = add(total, t + 1 + step, toward_near, lambda q: prod_f[k, q, a])
            out[e, a, r] = total.astype(jnp.bfloat16)
            return carry

        lax.fori_loop(0, atoms, body, 0)

    for r in range(parts):
        sent = set()
        for i in range(energies):
            if r == last and i == energies - 1:
                own_sums(r, (late,))
            if r == 0 and i == 0:
                coup_copy.wait()
                for copy in small:
                    copy.wait()
            @pl.when(has_left)
            def _(i=i, r=r):
                slab_copy(r, i, 0).wait_recv()
            @pl.when(has_right)
            def _(i=i, r=r):
                slab_copy(r, i, 1).wait_recv()

            def store(m, a, value, r=r, i=i):
                prod[m, r, step_at(r, i), a] = value

            products(wide[r][i], store, every)
            for side in range(2):
                done = set(orders[side][r][: i + 1])
                but = handed[: 2 - side] if r == last else ()
                for u in far_units(r):
                    wide_step = {u} - set(but)
                    others = {k for k in range(u - WID + 1, u) if k >= 0 and k not in but}
                    if (side, u) in sent or not wide_step | others <= done:
                        continue
                    sent.add((side, u))
                    @pl.when(has_far & (odd == side))
                    def _(u=u, r=r, but=but, others=others):
                        terms = [(q, u - WID + shift(q), toward_far(q)) for q in (every if others else every[:1])]
                        store_sum(far_send, r, u, terms, min(others, default=u), but)
                        energy_copy(r, u, 0).start()
                for u in reversed(range(WID)):
                    others = set(range(energies - WID + u + 1, energies))
                    if ("near", side, u) in sent or not {energies - WID + u} | others <= done:
                        continue
                    sent.add(("near", side, u))
                    @pl.when(has_near & (odd == side))
                    def _(u=u, r=r, others=others):
                        terms = [(q, energies + u - shift(q), toward_near(q)) for q in (every if others else every[:1])]
                        store_sum(near_send, r, u, terms, min(others, default=u))
                        energy_copy(r, u, 1).start()
            if r == last and i == 0:
                for k in range(2):
                    @pl.when(takes[k])
                    def _(k=k):
                        raw_copy(k).wait_recv()
                        @pl.when(has_right)
                        def _():
                            pass_copy(k, 0).start()
                        @pl.when(has_left)
                        def _():
                            pass_copy(k, 1).start()
        if r < last:
            own_sums(r)

    for r in range(last):
        for t in reversed(range(energies)):
            finish(r, t)

    for k in range(2):
        @pl.when(gives[k])
        def _(k=k):
            raw_copy(k).wait_send()
    @pl.when(has_far)
    def _():
        for r in range(last):
            for u in far_units(r):
                energy_copy(r, u, 0).wait_send()
    @pl.when(has_near)
    def _():
        for r in range(last):
            for u in range(WID):
                energy_copy(r, u, 1).wait_send()
    @pl.when(has_left)
    def _():
        for r in range(parts):
            for i in range(energies):
                slab_copy(r, i, 1).wait_send()
    @pl.when(has_right)
    def _():
        for r in range(parts):
            for i in range(energies):
                slab_copy(r, i, 0).wait_send()

    for k in range(2):
        @pl.when(takes[k])
        def _(k=k):
            @pl.when(has_left)
            def _():
                pass_copy(k, 0).wait_recv()
            @pl.when(has_right)
            def _():
                pass_copy(k, 1).wait_recv()

            def store(m, a, value):
                prod_f[k, m, a] = value

            products(foreign[k], store, every)

        @pl.when(jnp.logical_not(takes[k]))
        def _(k=k):
            prod_f[k] = jnp.zeros_like(prod_f[k])

    for t in reversed(range(energies)):
        finish(last, t)

    @pl.when(has_far)
    def _():
        for u in far_units(last):
            energy_copy(last, u, 0).wait_send()
    @pl.when(has_near)
    def _():
        for u in range(WID):
            energy_copy(last, u, 1).wait_send()
    for k in range(2):
        @pl.when(takes[k] & has_right)
        def _(k=k):
            pass_copy(k, 0).wait_send()
        @pl.when(takes[k] & has_left)
        def _(k=k):
            pass_copy(k, 1).wait_send()


def solution(mesh):
    def shards(green, coupling, neighbours, shifts, occupation):
        energies, atoms, parts, blk, _ = green.shape
        slots, modes = coupling.shape[1:3]
        sizes = (energies, atoms, parts, blk, slots, modes, mesh.shape["energy"], mesh.shape["slab"])
        bf16, f32 = jnp.bfloat16, jnp.float32
        hbm = pl.BlockSpec(memory_space=pltpu.HBM)
        edge = (parts, WID, atoms, blk, blk)
        dma = pltpu.SemaphoreType.DMA
        return pl.pallas_call(
            functools.partial(kernel, sizes),
            out_shape=pltpu.VMEM(green.shape, bf16),
            in_specs=[hbm] * 5,
            out_specs=pl.BlockSpec(memory_space=pltpu.VMEM),
            scratch_shapes=[pltpu.VMEM((atoms + 2 * HALO, blk, blk), bf16) for _ in range(parts * energies + 2)]
            + [
                pltpu.VMEM(coupling.shape, bf16),
                pltpu.VMEM((modes, parts, energies, atoms, blk, blk), bf16),
                pltpu.VMEM(edge, bf16),
                pltpu.VMEM(edge, bf16),
                pltpu.VMEM(edge, bf16),
                pltpu.VMEM(edge, bf16),
                pltpu.VMEM((parts, energies, atoms, blk, blk), f32),
                pltpu.SMEM((atoms, slots), jnp.int32),
                pltpu.SMEM((modes,), jnp.int32),
                pltpu.SMEM((modes,), f32),
                dma,
                dma((parts, energies)),
                dma((2, parts, energies)),
                dma((2, parts, energies)),
                dma((2, parts, WID)),
                dma((2, parts, WID)),
                dma((3,)),
                pltpu.VMEM((2, modes, atoms, blk, blk), bf16),
                dma((2,)),
                dma((2,)),
                dma((2, 2)),
                dma((2, 2)),
                pltpu.SemaphoreType.REGULAR,
                pltpu.SemaphoreType.REGULAR,
            ],
            compiler_params=pltpu.CompilerParams(collective_id=0, has_side_effects=True),
        )(neighbours, shifts, occupation, green, coupling)

    return jax.shard_map(
        shards,
        mesh=mesh,
        in_specs=(
            P("energy", "slab", None, None, None),
            P("slab", None, None, None, None),
            P("slab", None),
            P(),
            P(),
        ),
        out_specs=P("energy", "slab", None, None, None),
        check_vma=False,
    )
```
